128 devices in a mesh: sph: 16 (over z, y_lo, core), wave: 8 (over y_hi, x).
Axes of the slice: x: 4, y: 4 (y_hi: 2, y_lo: 2; y = y_hi * 2 + y_lo), z: 4, core: 2. Of those that a mesh axis runs over, the one named last changes fastest.
Arguments:
- coefficients: float32 [8, 96, 2048], P(None, None, 'sph'), may hold values from -6 to 6
- incident: float32 [8, 96, 2048], P(None, None, 'sph'), may hold values from -6 to 6
- positions: float32 [3, 2048], P(None, 'sph'), may hold values from 0 to 1
- neighbour_index: int32 [12, 2048], P(None, 'sph'), may hold values from 0 to 2047, as said below
- link_class: int32 [12, 2048], P(None, 'sph'), may hold values from 0 to 25
- link_count: int32 [2048], P('sph'), may hold values from 1 to 12, as said below
- sphere_type: int32 [2048], P('sph'), may hold values from 0 to 3
- translation: float32 [2, 26, 48, 48], replicated, may hold values from -0.1875 to 0.1875
- t_matrix: float32 [2, 4, 48, 48], replicated, may hold values from -0.375 to 0.375
- wave_grid: int32 [2, 4096], P(None, 'wave'), may hold values from -64 to 63
- vertical: float32 [4096], P('wave'), may hold values from 0.5 to 4
- expansion: float32 [2, 2, 48, 4096], P(None, None, None, 'wave'), may hold values from -0.013671875 to 0.013671875
- reflection: float32 [2, 2, 2, 4096], P(None, None, None, 'wave'), may hold values from -3 to 3
- projector: float32 [2, 48, 2, 4096], P(None, None, None, 'wave'), may hold values from -0.03125 to 0.03125
Outputs:
- updated: float32 [8, 96, 2048], P(None, None, 'sph')
The draws below stay inside these ranges and needn't reach their ends.
Inputs may be any that keep to these rules, and one draw needn't show every extreme that they name: `neighbour_index`: every entry lies within 128 of its own sphere's index; slots at or past link_count hold valid indices that are not used. `link_count`: the spheres of some aligned blocks of 128 have many more live slots than others.
All inputs are finite; a program needn't handle non-finite values.
Results may differ from the reference program's by a relative error of at most 0.0003.
Values sent between devices are 32-bit elements; how exact they have to be, the bound alone decides.
No kernel may reach another device: no remote copies, remote signals or barrier semaphores. Data moves between devices by JAX's collectives and lax.ppermute only.
A program may use at most 64 MiB of HBM per device.

```python
import math
import jax
import jax.numpy as jnp
from jax import lax

MODES = 48
ILLUMS = 8
LINKS = 12
OFFSETS = 26
TYPES = 4
GRID = 64
SPH_DEV = 128
WAVE_DEV = 512
SPHERES = 2048
WAVES = 4096
N_WAVE = 8


def draw_neighbour_index(key, part):
    spheres = lax.broadcasted_iota(jnp.int32, (LINKS, SPHERES), 1)
    slot_ids = lax.broadcasted_iota(jnp.int32, (LINKS, SPHERES), 0)
    offset = jax.random.randint(jax.random.fold_in(key, 11), (LINKS, SPHERES), -SPH_DEV, SPH_DEV + 1)
    target = jnp.clip(spheres + offset, 0, SPHERES - 1)
    target = jnp.where((slot_ids == 0) & (spheres == SPHERES - 1), SPHERES - 1, target)
    target = jnp.where((slot_ids == 0) & (spheres == 0), 0, target)
    return target.astype(jnp.int32)


def draw_link_count(key, part):
    blocks = SPHERES // SPH_DEV
    block_extra = jax.random.randint(jax.random.fold_in(key, 21), (blocks,), 0, 2 * LINKS)
    base_count = jax.random.randint(jax.random.fold_in(key, 22), (blocks, SPH_DEV), 1, LINKS + 1)
    link_total = jnp.minimum(base_count + block_extra[:, None] // 3, LINKS)
    position = lax.broadcasted_iota(jnp.int32, (blocks, SPH_DEV), 1)
    link_total = jnp.where(position == 0, LINKS, link_total)
    link_total = jnp.where(position == 1, 1, link_total)
    return link_total.reshape(SPHERES).astype(jnp.int32)


def place_ends(entries, own_key, low, top_value):
    index_at = [jax.random.randint(jax.random.fold_in(own_key, axis), (), 0, length) for axis, length in enumerate(entries.shape)]
    widest = entries.shape.index(max(entries.shape))
    next_to = index_at[:widest] + [(index_at[widest] + 1) % entries.shape[widest]] + index_at[widest + 1:]
    return entries.at[tuple(index_at)].set(low).at[tuple(next_to)].set(top_value)


def block_scale(stream_key, dims, cuts, low, top_value):
    factor_of, own = 1.0, jax.random.fold_in(stream_key, 6)
    for dim, blocks in cuts:
        steps = jnp.exp(jax.random.uniform(jax.random.fold_in(own, dim), (blocks,), jnp.float32, low / len(cuts), top_value / len(cuts)))
        factor_of = factor_of * jnp.repeat(steps, dims[dim] // blocks).reshape([-1 if axis == dim else 1 for axis in range(len(dims))])
    return factor_of


def gaussian(stream_key, dims, width, reach, cuts=(), dtype=jnp.bfloat16):
    values = width * jax.random.normal(stream_key, dims, jnp.float32)
    if cuts:
        values = values * block_scale(stream_key, dims, cuts, -0.22, 0.18)
    return jnp.clip(values, -reach, reach).astype(dtype)


def setup_inputs(seed: int = 0) -> dict:
    key_list = jax.random.split(jax.random.key(seed), 15)
    return {
        "coefficients": gaussian(key_list[0], (ILLUMS, 2 * MODES, SPHERES), 1.0, 6.0, ((2, 16),), jnp.float32),
        "incident": gaussian(key_list[1], (ILLUMS, 2 * MODES, SPHERES), 1.0, 6.0, ((2, 16),), jnp.float32),
        "positions": jnp.clip(1.0 * jax.random.uniform(key_list[2], (3, SPHERES), jnp.float32) ** block_scale(key_list[2], (3, SPHERES), ((1, 16),), -0.2, 0.2), 0.0, 1.0),
        "neighbour_index": draw_neighbour_index(jax.random.fold_in(key_list[14], 71), 0),
        "link_class": place_ends(jax.random.randint(key_list[4], (LINKS, SPHERES), 0, OFFSETS), jax.random.fold_in(key_list[4], 1), 0, OFFSETS - 1).astype(jnp.int32),
        "link_count": draw_link_count(jax.random.fold_in(key_list[14], 71), 0),
        "sphere_type": place_ends(jax.random.randint(key_list[6], (SPHERES,), 0, TYPES), jax.random.fold_in(key_list[6], 1), 0, TYPES - 1).astype(jnp.int32),
        "translation": gaussian(key_list[7], (2, OFFSETS, MODES, MODES), (2 * MODES * LINKS) ** -0.5, 0.1875, (), jnp.float32),
        "t_matrix": gaussian(key_list[8], (2, TYPES, MODES, MODES), (6 * MODES) ** -0.5, 0.375, (), jnp.float32),
        "wave_grid": place_ends(jax.random.randint(key_list[9], (2, WAVES), -GRID, GRID), jax.random.fold_in(key_list[9], 1), -GRID, GRID - 1).astype(jnp.int32),
        "vertical": jnp.clip(jnp.exp(math.log(4.0) - 2.0794415 * jax.random.uniform(key_list[10], (WAVES,), jnp.float32) ** block_scale(key_list[10], (WAVES,), ((0, 8),), -0.2, 0.2)), 0.5, 4.0),
        "expansion": gaussian(key_list[11], (2, 2, MODES, WAVES), (2 * MODES * SPHERES) ** -0.5, 0.013671875, ((3, 8),), jnp.float32),
        "reflection": gaussian(key_list[12], (2, 2, 2, WAVES), 0.5, 3.0, ((3, 8),), jnp.float32),
        "projector": gaussian(key_list[13], (2, MODES, 2, WAVES), (8 * WAVES) ** -0.5, 0.03125, ((3, 8),), jnp.float32),
    }


PRECISE = lax.Precision.HIGHEST
TWO_PI = 6.283185307179586


def realify(complex_pair):
    upper_half = jnp.concatenate([complex_pair[0], -complex_pair[1]], axis=-1)
    lower_half = jnp.concatenate([complex_pair[1], complex_pair[0]], axis=-1)
    return jnp.concatenate([upper_half, lower_half], axis=-2)


def contract(form, left, right):
    return jnp.einsum(form, left, right, precision=PRECISE)


def translate(source, index, link_class, link_count, translation):
    illums = source.shape[0]
    link_slots = index.shape[0]
    spheres = index.shape[1]
    picked = jnp.take(source, index.reshape(-1), axis=2).reshape(illums, 2 * MODES, link_slots, spheres)
    slot_ids = lax.broadcasted_iota(jnp.int32, index.shape, 0)
    live_links = (slot_ids < link_count[None, :]).astype(jnp.float32)
    class_ids = lax.broadcasted_iota(jnp.int32, (OFFSETS,) + index.shape, 0)
    weights = jnp.where(class_ids == link_class[None], live_links[None], jnp.zeros_like(live_links)[None])
    binned = contract("bjks,cks->cjbs", picked, weights)
    operator_rows = jnp.transpose(realify(translation), (1, 0, 2)).reshape(2 * MODES, OFFSETS * 2 * MODES)
    translated = jnp.dot(operator_rows, binned.reshape(OFFSETS * 2 * MODES, illums * spheres), precision=PRECISE, preferred_element_type=jnp.float32)
    return translated.reshape(2 * MODES, illums, spheres)


def angles(positions, wave_ids, vertical):
    across = wave_ids[0].astype(jnp.float32)
    along = wave_ids[1].astype(jnp.float32)
    plane_angle = TWO_PI * (positions[0][:, None] * across[None, :] + positions[1][:, None] * along[None, :])
    height_angle = positions[2][:, None] * vertical[None, :]
    return plane_angle, height_angle


def expand(coefficients, positions, wave_ids, vertical, expansion):
    illums = coefficients.shape[0]
    waves = wave_ids.shape[1]
    plane_angle, height_angle = angles(positions, wave_ids, vertical)
    down_angle = plane_angle - height_angle
    phase_tiles = jnp.concatenate([jnp.cos(down_angle), jnp.sin(down_angle)], axis=1)
    products = jnp.dot(coefficients.reshape(illums * 2 * MODES, -1), phase_tiles, precision=PRECISE, preferred_element_type=jnp.float32)
    products = products.reshape(illums, 2, MODES, 2, waves)
    spec_real = products[:, 0, :, 0] + products[:, 1, :, 1]
    spec_imag = products[:, 1, :, 0] - products[:, 0, :, 1]
    out_real = contract("plw,blw->bpw", expansion[0], spec_real) - contract("plw,blw->bpw", expansion[1], spec_imag)
    out_imag = contract("plw,blw->bpw", expansion[0], spec_imag) + contract("plw,blw->bpw", expansion[1], spec_real)
    return jnp.stack([out_real, out_imag], axis=1)


def reflect(spectrum, reflection):
    spec_real = spectrum[:, 0]
    spec_imag = spectrum[:, 1]
    out_real = contract("pqw,bqw->bpw", reflection[0], spec_real) - contract("pqw,bqw->bpw", reflection[1], spec_imag)
    out_imag = contract("pqw,bqw->bpw", reflection[0], spec_imag) + contract("pqw,bqw->bpw", reflection[1], spec_real)
    return jnp.stack([out_real, out_imag], axis=1)


def wave_field(reflected, projector):
    spec_real = reflected[:, 0]
    spec_imag = reflected[:, 1]
    field_real = contract("lpw,bpw->blw", projector[0], spec_real) - contract("lpw,bpw->blw", projector[1], spec_imag)
    field_imag = contract("lpw,bpw->blw", projector[0], spec_imag) + contract("lpw,bpw->blw", projector[1], spec_real)
    return jnp.stack([field_real, field_imag], axis=1)


def up_tiles(positions, wave_ids, vertical):
    plane_angle, height_angle = angles(positions, wave_ids, vertical)
    up_angle = plane_angle + height_angle
    return jnp.concatenate([jnp.cos(up_angle), jnp.sin(up_angle)], axis=0)


def project(spectral_field, phase_tiles):
    illums = spectral_field.shape[0]
    spheres = phase_tiles.shape[0] // 2
    products = lax.dot_general(spectral_field.reshape(illums * 2 * MODES, -1), phase_tiles, (((1,), (1,)), ((), ())), precision=PRECISE, preferred_element_type=jnp.float32)
    products = products.reshape(illums, 2, MODES, 2, spheres)
    resp_real = products[:, 0, :, 0] - products[:, 1, :, 1]
    resp_imag = products[:, 0, :, 1] + products[:, 1, :, 0]
    return jnp.stack([resp_real, resp_imag], axis=1).reshape(illums, 2 * MODES, spheres)


def apply_types(exciting, sphere_type, t_matrix):
    operator_rows = realify(t_matrix).reshape(TYPES * 2 * MODES, 2 * MODES)
    all_types = jnp.dot(operator_rows, exciting.reshape(2 * MODES, -1), precision=PRECISE, preferred_element_type=jnp.float32)
    all_types = all_types.reshape(TYPES, 2 * MODES, exciting.shape[1], exciting.shape[2])
    type_ids = lax.broadcasted_iota(jnp.int32, (TYPES, exciting.shape[2]), 0)
    type_weights = (type_ids == sphere_type[None, :]).astype(jnp.float32)
    return jnp.sum(all_types * type_weights[:, None, None, :], axis=0)


def reference(coefficients, incident, positions, neighbour_index, link_class, link_count, sphere_type, translation, t_matrix, wave_grid, vertical, expansion, reflection, projector):
    translated = translate(coefficients, neighbour_index, link_class, link_count, translation)

    def blocked(array):
        leading = array.shape[:-1]
        return jnp.moveaxis(array.reshape(leading + (N_WAVE, WAVE_DEV)), -2, 0)

    def wave_block_step(summed, pieces):
        wave_ids, vertical_block, expansion_block, reflection_block, projector_block = pieces
        spectrum = expand(coefficients, positions, wave_ids, vertical_block, expansion_block)
        reflected = reflect(spectrum, reflection_block)
        phase_tiles = up_tiles(positions, wave_ids, vertical_block)
        return summed + project(wave_field(reflected, projector_block), phase_tiles), None

    start_value = jnp.zeros(coefficients.shape, jnp.float32)
    response, unused = lax.scan(wave_block_step, start_value, (blocked(wave_grid), blocked(vertical), blocked(expansion), blocked(reflection), blocked(projector)))
    exciting = jnp.transpose(incident + response, (1, 0, 2)) + translated
    return jnp.transpose(apply_types(exciting, sphere_type, t_matrix), (1, 0, 2))
```

```python
import jax
import jax.numpy as jnp
from jax import lax
from jax.experimental import pallas as pl
from jax.experimental.pallas import tpu as pltpu
from jax.sharding import PartitionSpec as P

MODES = 48
OFFSETS = 26
TYPES = 4
LINKS = 12
INV_TWO_PI = 0.15915494309189535

SIN_POLY = (3.14159264, -5.16771008, 2.55007752, -0.59829129, 0.07765766)
COS_POLY = (1.0, -4.93480214, 4.05870916, -1.335212, 0.23493731, -0.02439632)

VMEM = pl.BlockSpec(memory_space=pltpu.VMEM)
SMEM = pl.BlockSpec(memory_space=pltpu.SMEM)
BF16 = jnp.bfloat16
F32 = jnp.float32


def horner(coefs, t):
    acc = coefs[-1] * t + coefs[-2]
    for value in coefs[-3::-1]:
        acc = acc * t + value
    return acc


def cos_sin_turns(turns):
    rest = turns - jnp.round(turns)
    t = rest * rest
    s = rest * horner(SIN_POLY, t)
    c = horner(COS_POLY, t)
    return 1.0 - 2.0 * (s * s), 2.0 * (s * c)


def split(x):
    hi = x.astype(BF16)
    return hi, (x - hi.astype(F32)).astype(BF16)


def dot3(ah, al, bh, bl):
    def dot(a, b):
        return jnp.dot(a, b, preferred_element_type=F32)

    return dot(ah, bh) + (dot(ah, bl) + dot(al, bh))


def columns(rows):
    pad = jnp.zeros((8 - rows.shape[0], rows.shape[1]), F32)
    return jnp.concatenate([rows, pad], axis=0).T


def expand_kernel(flip_ref, coef_ref, pos_ref, grid_ref, vert_ref, exp_ref, out_ref, ah, al, spec):
    illums = coef_ref.shape[0]
    waves = grid_ref.shape[1]
    half = illums * MODES
    for b in range(illums):
        block = coef_ref[jnp.bitwise_xor(flip_ref[0], b)]
        re, im = block[:MODES], block[MODES:]
        for base, left, right in ((0, re, im), (half, im, -re)):
            rows = pl.ds(base + b * MODES, MODES)
            for offset, part in ((0, left), (128, right)):
                hi, lo = split(part)
                ah[rows, offset : offset + 128] = hi
                al[rows, offset : offset + 128] = lo
    pos = columns(pos_ref[...])
    grid = grid_ref[...].astype(F32)
    vert = vert_ref[...].reshape(1, waves) * INV_TWO_PI
    width = 256
    for start in range(0, waves, width):
        lanes = slice(start, start + width)
        turns = pos[:, 0:1] * grid[0:1, lanes] + pos[:, 1:2] * grid[1:2, lanes]
        turns = turns - pos[:, 2:3] * vert[:, lanes]
        cos, sin = cos_sin_turns(turns)
        bh, bl = split(jnp.concatenate([cos, sin], axis=0))
        spec[...] = dot3(ah[...], al[...], bh, bl)
        for p in range(2):
            er, ei = exp_ref[0, p, :, lanes], exp_ref[1, p, :, lanes]
            out_re, out_im = [], []
            for b in range(illums):
                sr = spec[b * MODES : (b + 1) * MODES, :]
                si = spec[half + b * MODES : half + (b + 1) * MODES, :]
                out_re.append(jnp.sum(er * sr - ei * si, axis=0, keepdims=True))
                out_im.append(jnp.sum(er * si + ei * sr, axis=0, keepdims=True))
            out_ref[2 * p, :, lanes] = jnp.concatenate(out_re, axis=0)
            out_ref[2 * p + 1, :, lanes] = jnp.concatenate(out_im, axis=0)


def expand(flip, coefficients, positions, wave_grid, vertical, expansion):
    illums, _, spheres = coefficients.shape
    waves = wave_grid.shape[1]
    rows = illums * 2 * MODES
    return pl.pallas_call(
        expand_kernel,
        name="expand",
        out_shape=jax.ShapeDtypeStruct((4, illums, waves), F32),
        in_specs=[SMEM] + [VMEM] * 5,
        out_specs=VMEM,
        scratch_shapes=[
            pltpu.VMEM((rows, 2 * spheres), BF16),
            pltpu.VMEM((rows, 2 * spheres), BF16),
            pltpu.VMEM((rows, 256), F32),
        ],
        cost_estimate=pl.CostEstimate(
            flops=6 * rows * 2 * spheres * waves, bytes_accessed=4 << 20, transcendentals=0
        ),
    )(flip, coefficients, positions, wave_grid, vertical, expansion)


def prepare_kernel(pos_ref, grid_ref, vert_ref, refl_ref, proj_ref, uh, ul, qr_ref):
    waves = grid_ref.shape[1]
    spheres = pos_ref.shape[1]
    grid = grid_ref[...].astype(F32)
    vert = vert_ref[...].reshape(1, waves) * INV_TWO_PI
    cols = columns(jnp.concatenate([grid, vert], axis=0))
    turns = cols[:, 0:1] * pos_ref[0:1, :] + cols[:, 1:2] * pos_ref[1:2, :]
    turns = turns + cols[:, 2:3] * pos_ref[2:3, :]
    cos, sin = cos_sin_turns(turns)
    ch, cl = split(cos)
    sh, sl = split(sin)
    for ref, c, s in ((uh, ch, sh), (ul, cl, sl)):
        ref[:waves, :spheres] = c
        ref[:waves, spheres:] = s
        ref[waves:, :spheres] = -s
        ref[waves:, spheres:] = c
    for q in range(2):
        acc_re = acc_im = None
        for p in range(2):
            pr, pi = proj_ref[0, :, p, :], proj_ref[1, :, p, :]
            rr = refl_ref[0, p, q : q + 1, :]
            ri = refl_ref[1, p, q : q + 1, :]
            term_re = pr * rr - pi * ri
            term_im = pr * ri + pi * rr
            acc_re = term_re if acc_re is None else acc_re + term_re
            acc_im = term_im if acc_im is None else acc_im + term_im
        qr_ref[2 * q] = acc_re
        qr_ref[2 * q + 1] = acc_im


def prepare(positions, wave_grid, vertical, reflection, projector):
    waves = wave_grid.shape[1]
    spheres = positions.shape[1]
    tiles = jax.ShapeDtypeStruct((2 * waves, 2 * spheres), BF16)
    return pl.pallas_call(
        prepare_kernel,
        name="prepare",
        out_shape=(tiles, tiles, jax.ShapeDtypeStruct((4, MODES, waves), F32)),
        in_specs=[VMEM] * 5,
        out_specs=(VMEM,) * 3,
        cost_estimate=pl.CostEstimate(
            flops=2 << 20, bytes_accessed=2 << 20, transcendentals=0
        ),
    )(positions, wave_grid, vertical, reflection, projector)


def project_kernel(mine_ref, other_ref, qr_ref, uh, ul, *refs):
    outs, (fh, fl) = refs[:-2], refs[-2:]
    illums = mine_ref.shape[1]
    waves = mine_ref.shape[2]
    width = 128
    for start in range(0, waves, width):
        lanes = slice(start, start + width)
        spec = [mine_ref[i, :, lanes] + other_ref[i, :, lanes] for i in range(4)]
        qr = [qr_ref[i, :, lanes] for i in range(4)]
        for b in range(illums):
            rows = slice(b * MODES, (b + 1) * MODES)
            x = [part[b : b + 1, :] for part in spec]
            fr = (qr[0] * x[0] - qr[1] * x[1]) + (qr[2] * x[2] - qr[3] * x[3])
            fi = (qr[0] * x[1] + qr[1] * x[0]) + (qr[2] * x[3] + qr[3] * x[2])
            for base, part in ((0, fr), (waves, fi)):
                hi, lo = split(part)
                fh[rows, base + start : base + start + width] = hi
                fl[rows, base + start : base + start + width] = lo
    out = dot3(fh[...], fl[...], uh[...], ul[...])
    per_piece = illums // len(outs)
    for b in range(illums):
        ref = outs[b // per_piece]
        rows = out[b * MODES : (b + 1) * MODES]
        ref[b % per_piece, :MODES, :] = rows[:, :128]
        ref[b % per_piece, MODES:, :] = rows[:, 128:]


def project(mine, other, qr, uh, ul, pieces):
    illums, waves = mine.shape[1:]
    spheres = uh.shape[1] // 2
    piece = jax.ShapeDtypeStruct((illums // pieces, 2 * MODES, spheres), F32)
    return pl.pallas_call(
        project_kernel,
        name="project",
        out_shape=(piece,) * pieces,
        in_specs=[VMEM] * 5,
        out_specs=(VMEM,) * pieces,
        scratch_shapes=[pltpu.VMEM((illums * MODES, 2 * waves), BF16)] * 2,
        cost_estimate=pl.CostEstimate(
            flops=6 * illums * MODES * 2 * waves * 2 * spheres,
            bytes_accessed=3 << 20,
            transcendentals=0,
        ),
    )(mine, other, qr, uh, ul)


def translate_kernel(
    where_ref, low_ref, own_ref, high_ref, inc_ref, idx_ref, class_ref, count_ref, trans_ref, out_ref, bh, bl, gh, gl
):
    own = where_ref[0]
    slot = where_ref[1]
    base = where_ref[2]
    spheres = own_ref.shape[2]
    local = idx_ref[...] - base
    side = jnp.right_shift(local, 7)
    lane = jnp.bitwise_and(local, 127)
    live = lax.broadcasted_iota(jnp.int32, local.shape, 0) < count_ref[...].reshape(1, spheres)
    kind = jnp.where(live, class_ref[...], OFFSETS)
    source = (low_ref[0], own_ref[own], high_ref[0])
    shape = (2 * MODES, spheres)
    picked = []
    for k in range(LINKS):
        at = jnp.broadcast_to(lane[k : k + 1, :], shape)
        got = [jnp.take_along_axis(x, at, axis=1) for x in source]
        pick = jnp.where(side[k : k + 1, :] == 0, got[0], got[2])
        picked.append(jnp.where(side[k : k + 1, :] == 1, got[1], pick))
    for c in range(OFFSETS):
        total = None
        for k in range(LINKS):
            term = jnp.where(kind[k : k + 1, :] == c, picked[k], 0.0)
            total = term if total is None else total + term
        hi, lo = split(total)
        rows = slice(c * MODES, (c + 1) * MODES)
        for ref, part in ((bh, hi), (bl, lo)):
            ref[rows, :spheres] = part[:MODES]
            ref[rows, spheres:] = part[MODES:]
        hi, lo = split(jnp.concatenate([trans_ref[0, c], trans_ref[1, c]], axis=0))
        gh[:, rows] = hi
        gl[:, rows] = lo
    both = dot3(gh[...], gl[...], bh[...], bl[...])
    upper, lower = both[:MODES], both[MODES:]
    result = jnp.concatenate(
        [upper[:, :spheres] - lower[:, spheres:], upper[:, spheres:] + lower[:, :spheres]], axis=0
    )
    result = result + inc_ref[own]
    out_ref[0] = jnp.where(slot == 0, result, 0.0)
    out_ref[1] = jnp.where(slot == 0, 0.0, result)


def translate(where, low, coefficients, high, incident, index, link_class, link_count, translation):
    spheres = index.shape[1]
    return pl.pallas_call(
        translate_kernel,
        name="translate",
        out_shape=jax.ShapeDtypeStruct((2, 2 * MODES, spheres), F32),
        in_specs=[SMEM] + [VMEM] * 8,
        out_specs=VMEM,
        scratch_shapes=[
            pltpu.VMEM((OFFSETS * MODES, 2 * spheres), BF16),
            pltpu.VMEM((OFFSETS * MODES, 2 * spheres), BF16),
            pltpu.VMEM((2 * MODES, OFFSETS * MODES), BF16),
            pltpu.VMEM((2 * MODES, OFFSETS * MODES), BF16),
        ],
        cost_estimate=pl.CostEstimate(
            flops=6 * 2 * MODES * OFFSETS * MODES * 2 * spheres,
            bytes_accessed=2 << 20,
            transcendentals=0,
        ),
    )(where, low, coefficients, high, incident, index, link_class, link_count, translation)


def types_kernel(mine_ref, other_ref, type_ref, tmat_ref, out_ref, th, tl):
    count = mine_ref.shape[0]
    spheres = mine_ref.shape[2]
    for t in range(TYPES):
        hi, lo = split(jnp.concatenate([tmat_ref[0, t], tmat_ref[1, t]], axis=0))
        th[:, t * MODES : (t + 1) * MODES] = hi
        tl[:, t * MODES : (t + 1) * MODES] = lo
    kind = type_ref[...].reshape(1, spheres)
    for b in range(count):
        x = mine_ref[b] + other_ref[b]
        wide = jnp.concatenate([x[:MODES], x[MODES:]], axis=1)
        kinds = jnp.concatenate([kind, kind], axis=1)
        stacked = jnp.concatenate(
            [jnp.where(kinds == t, wide, 0.0) for t in range(TYPES)], axis=0
        )
        bh, bl = split(stacked)
        both = dot3(th[...], tl[...], bh, bl)
        upper, lower = both[:MODES], both[MODES:]
        out_ref[b, :MODES, :] = upper[:, :spheres] - lower[:, spheres:]
        out_ref[b, MODES:, :] = upper[:, spheres:] + lower[:, :spheres]


def apply_types(mine, other, sphere_type, t_matrix):
    return pl.pallas_call(
        types_kernel,
        name="types",
        out_shape=jax.ShapeDtypeStruct(mine.shape, F32),
        in_specs=[VMEM] * 4,
        out_specs=VMEM,
        scratch_shapes=[pltpu.VMEM((2 * MODES, TYPES * MODES), BF16)] * 2,
        cost_estimate=pl.CostEstimate(
            flops=6 * 2 * MODES * TYPES * MODES * 4 * 128, bytes_accessed=1 << 20, transcendentals=0
        ),
    )(mine, other, sphere_type, t_matrix)


def swap(x, axis, mask):
    return lax.ppermute(x, axis, [(i, i ^ mask) for i in range(lax.axis_size(axis))])


def per_device(
    coefficients,
    incident,
    positions,
    neighbour_index,
    link_class,
    link_count,
    sphere_type,
    translation,
    t_matrix,
    wave_grid,
    vertical,
    expansion,
    reflection,
    projector,
):
    block = coefficients.shape[2]
    sph = lax.axis_index("sph")
    wave = lax.axis_index("wave")
    along_x = jnp.bitwise_and(wave, 3)
    slot = jnp.right_shift(wave, 2)
    own = 2 * along_x + slot
    flip = (2 * along_x)[None]
    where = jnp.stack([own, slot, (sph - 1) * block])

    count = lax.axis_size("sph")
    own_coefs = lax.dynamic_slice_in_dim(coefficients, own, 1, 0)
    up = [(i, i + 1) for i in range(count - 1)]
    down = [(i + 1, i) for i in range(count - 1)]
    low = lax.ppermute(own_coefs, "sph", up)
    high = lax.ppermute(own_coefs, "sph", down)

    part = expand(flip, coefficients, positions, wave_grid, vertical, expansion)
    part = part + swap(part, "sph", 1)
    part = (part + swap(part, "sph", 6)) + (swap(part, "sph", 2) + swap(part, "sph", 4))
    other = swap(part, "sph", 12)

    uh, ul, qr = prepare(positions, wave_grid, vertical, reflection, projector)
    translated = translate(
        where, low, coefficients, high, incident, neighbour_index, link_class, link_count, translation
    )
    keep, to1, to2, to3 = project(part, other, qr, uh, ul, 4)
    got2, got1, got3 = swap(to2, "wave", 2), swap(to1, "wave", 1), swap(to3, "wave", 3)
    summed = ((keep + translated) + got1) + (got2 + got3)
    across = swap(summed, "wave", 4)
    updated = apply_types(summed, across, sphere_type, t_matrix)
    from2, from1, from3 = swap(updated, "wave", 2), swap(updated, "wave", 1), swap(updated, "wave", 3)
    pieces = (updated, from1, from2, from3)

    def pick(group):
        near = jnp.where(along_x == group, pieces[0], pieces[1])
        far = jnp.where(along_x == (group ^ 2), pieces[2], pieces[3])
        is_near = jnp.right_shift(along_x, 1) == (group >> 1)
        return jnp.where(is_near, near, far)

    return jnp.concatenate([pick(group) for group in range(4)], axis=0)


def solution(mesh):
    placed = (
        P(None, None, "sph"),
        P(None, None, "sph"),
        P(None, "sph"),
        P(None, "sph"),
        P(None, "sph"),
        P("sph"),
        P("sph"),
        P(),
        P(),
        P(None, "wave"),
        P("wave"),
        P(None, None, None, "wave"),
        P(None, None, None, "wave"),
        P(None, None, None, "wave"),
    )
    return jax.shard_map(
        per_device, mesh=mesh, in_specs=placed, out_specs=P(None, None, "sph"), check_vma=False
    )
```

```python
import jax
import jax.numpy as jnp
from jax import lax
from jax.experimental import pallas as pl
from jax.experimental.pallas import tpu as pltpu
from jax.sharding import PartitionSpec as P


MODES = 48
OFFSETS = 26
TYPES = 4
LINKS = 12
INV_TWO_PI = 0.15915494309189535

SIN_POLY = (3.14159264, -5.16771008, 2.55007752, -0.59829129, 0.07765766)
COS_POLY = (1.0, -4.93480214, 4.05870916, -1.335212, 0.23493731, -0.02439632)

VMEM = pl.BlockSpec(memory_space=pltpu.VMEM)
HBM = pl.BlockSpec(memory_space=pltpu.HBM)
SMEM = pl.BlockSpec(memory_space=pltpu.SMEM)
BF16 = jnp.bfloat16
F32 = jnp.float32
PARAMS = pltpu.CompilerParams(vmem_limit_bytes=12 << 20)


def horner(coefs, t):
    acc = coefs[-1] * t + coefs[-2]
    for value in coefs[-3::-1]:
        acc = acc * t + value
    return acc


def cos_sin_turns(turns):
    rest = turns - jnp.round(turns)
    t = rest * rest
    s = rest * horner(SIN_POLY, t)
    c = horner(COS_POLY, t)
    return 1.0 - 2.0 * (s * s), 2.0 * (s * c)


def split(x):
    hi = x.astype(BF16)
    return hi, (x - hi.astype(F32)).astype(BF16)


def dot3(ah, al, bh, bl):
    def dot(a, b):
        return jnp.dot(a, b, preferred_element_type=F32)

    return dot(ah, bh) + (dot(ah, bl) + dot(al, bh))


def columns(rows):
    pad = jnp.zeros((8 - rows.shape[0], rows.shape[1]), F32)
    return jnp.concatenate([rows, pad], axis=0).T


def expand_kernel(
    flip_ref,
    own_ref,
    coef_hbm,
    pos_hbm,
    grid_hbm,
    vert_hbm,
    exp_hbm,
    out_ref,
    mine_ref,
    coef_ref,
    pos_ref,
    grid_ref,
    vert_ref,
    exp_ref,
    ah,
    al,
    spec,
    sems,
):
    copies = [
        pltpu.make_async_copy(source, target, sems.at[i])
        for i, (source, target) in enumerate(
            (
                (pos_hbm, pos_ref),
                (grid_hbm, grid_ref),
                (vert_hbm, vert_ref),
                (coef_hbm, coef_ref),
                (exp_hbm, exp_ref),
            )
        )
    ]
    for copy in copies:
        copy.start()
    illums = coef_ref.shape[0]
    waves = grid_ref.shape[1]
    half = illums * MODES
    for copy in copies[:3]:
        copy.wait()
    pos = columns(pos_ref[...])
    grid = grid_ref[...].astype(F32)
    vert = vert_ref[...].reshape(1, waves) * INV_TWO_PI
    turns = pos[:, 0:1] * grid[0:1] + pos[:, 1:2] * grid[1:2] - pos[:, 2:3] * vert
    cos, sin = cos_sin_turns(turns)
    bh, bl = split(jnp.concatenate([cos, sin], axis=0))
    copies[3].wait()
    mine_ref[0] = coef_ref[own_ref[0]]
    for b in range(illums):
        block = coef_ref[jnp.bitwise_xor(flip_ref[0], b)]
        re, im = block[:MODES], block[MODES:]
        for base, left, right in ((0, re, im), (half, im, -re)):
            rows = pl.ds(base + b * MODES, MODES)
            for offset, part in ((0, left), (128, right)):
                hi, lo = split(part)
                ah[rows, offset : offset + 128] = hi
                al[rows, offset : offset + 128] = lo
    copies[4].wait()
    width = 256
    for start in range(0, waves, width):
        lanes = slice(start, start + width)
        spec[...] = dot3(ah[...], al[...], bh[:, lanes], bl[:, lanes])
        for p in range(2):
            er, ei = exp_ref[0, p, :, lanes], exp_ref[1, p, :, lanes]
            out_re, out_im = [], []
            for b in range(illums):
                sr = spec[b * MODES : (b + 1) * MODES, :]
                si = spec[half + b * MODES : half + (b + 1) * MODES, :]
                out_re.append(jnp.sum(er * sr - ei * si, axis=0, keepdims=True))
                out_im.append(jnp.sum(er * si + ei * sr, axis=0, keepdims=True))
            out_ref[2 * p, :, lanes] = jnp.concatenate(out_re, axis=0)
            out_ref[2 * p + 1, :, lanes] = jnp.concatenate(out_im, axis=0)


def expand(flip, own, coefficients, positions, wave_grid, vertical, expansion):
    illums, _, spheres = coefficients.shape
    waves = wave_grid.shape[1]
    rows = illums * 2 * MODES
    arrays = (coefficients, positions, wave_grid, vertical, expansion)
    return pl.pallas_call(
        expand_kernel,
        name="expand",
        out_shape=(
            jax.ShapeDtypeStruct((4, illums, waves), F32),
            jax.ShapeDtypeStruct((1, 2 * MODES, spheres), F32),
        ),
        in_specs=[SMEM] * 2 + [HBM] * 5,
        out_specs=(VMEM, VMEM),
        scratch_shapes=[pltpu.VMEM(x.shape, x.dtype) for x in arrays]
        + [
            pltpu.VMEM((rows, 2 * spheres), BF16),
            pltpu.VMEM((rows, 2 * spheres), BF16),
            pltpu.VMEM((rows, 256), F32),
            pltpu.SemaphoreType.DMA((5,)),
        ],
        compiler_params=PARAMS,
        cost_estimate=pl.CostEstimate(
            flops=6 * rows * 2 * spheres * waves, bytes_accessed=4 << 20, transcendentals=0
        ),
    )(flip, own, *(pltpu.with_memory_space_constraint(x, pltpu.HBM) for x in arrays))


def prepare_kernel(pos_ref, grid_ref, vert_ref, refl_ref, proj_ref, tmat_ref, uh, ul, qr_ref, th, tl):
    for t in range(TYPES):
        hi, lo = split(jnp.concatenate([tmat_ref[0, t], tmat_ref[1, t]], axis=0))
        th[:, t * MODES : (t + 1) * MODES] = hi
        tl[:, t * MODES : (t + 1) * MODES] = lo
    waves = grid_ref.shape[1]
    spheres = pos_ref.shape[1]
    grid = grid_ref[...].astype(F32)
    vert = vert_ref[...].reshape(1, waves) * INV_TWO_PI
    cols = columns(jnp.concatenate([grid, vert], axis=0))
    turns = cols[:, 0:1] * pos_ref[0:1, :] + cols[:, 1:2] * pos_ref[1:2, :]
    turns = turns + cols[:, 2:3] * pos_ref[2:3, :]
    cos, sin = cos_sin_turns(turns)
    ch, cl = split(cos)
    sh, sl = split(sin)
    for ref, c, s in ((uh, ch, sh), (ul, cl, sl)):
        ref[:waves, :spheres] = c
        ref[:waves, spheres:] = s
        ref[waves:, :spheres] = -s
        ref[waves:, spheres:] = c
    for q in range(2):
        acc_re = acc_im = None
        for p in range(2):
            pr, pi = proj_ref[0, :, p, :], proj_ref[1, :, p, :]
            rr = refl_ref[0, p, q : q + 1, :]
            ri = refl_ref[1, p, q : q + 1, :]
            term_re = pr * rr - pi * ri
            term_im = pr * ri + pi * rr
            acc_re = term_re if acc_re is None else acc_re + term_re
            acc_im = term_im if acc_im is None else acc_im + term_im
        qr_ref[2 * q] = acc_re
        qr_ref[2 * q + 1] = acc_im


def prepare(positions, wave_grid, vertical, reflection, projector, t_matrix):
    waves = wave_grid.shape[1]
    spheres = positions.shape[1]
    tiles = jax.ShapeDtypeStruct((2 * waves, 2 * spheres), BF16)
    types = jax.ShapeDtypeStruct((2 * MODES, TYPES * MODES), BF16)
    return pl.pallas_call(
        prepare_kernel,
        name="prepare",
        out_shape=(tiles, tiles, jax.ShapeDtypeStruct((4, MODES, waves), F32), types, types),
        in_specs=[VMEM] * 6,
        out_specs=(VMEM,) * 5,
        compiler_params=PARAMS,
        cost_estimate=pl.CostEstimate(
            flops=2 << 20, bytes_accessed=2 << 20, transcendentals=0
        ),
    )(positions, wave_grid, vertical, reflection, projector, t_matrix)


def project_kernel(mine_ref, other_ref, qr_ref, uh, ul, *refs):
    outs, (fh, fl) = refs[:-2], refs[-2:]
    illums = mine_ref.shape[1]
    waves = mine_ref.shape[2]
    width = 128
    for start in range(0, waves, width):
        lanes = slice(start, start + width)
        spec = [mine_ref[i, :, lanes] + other_ref[i, :, lanes] for i in range(4)]
        qr = [qr_ref[i, :, lanes] for i in range(4)]
        for b in range(illums):
            rows = slice(b * MODES, (b + 1) * MODES)
            x = [part[b : b + 1, :] for part in spec]
            fr = (qr[0] * x[0] - qr[1] * x[1]) + (qr[2] * x[2] - qr[3] * x[3])
            fi = (qr[0] * x[1] + qr[1] * x[0]) + (qr[2] * x[3] + qr[3] * x[2])
            for base, part in ((0, fr), (waves, fi)):
                hi, lo = split(part)
                fh[rows, base + start : base + start + width] = hi
                fl[rows, base + start : base + start + width] = lo
    out = dot3(fh[...], fl[...], uh[...], ul[...])
    per_piece = illums // len(outs)
    for b in range(illums):
        ref = outs[b // per_piece]
        rows = out[b * MODES : (b + 1) * MODES]
        ref[b % per_piece, :MODES, :] = rows[:, :128]
        ref[b % per_piece, MODES:, :] = rows[:, 128:]


def project(mine, other, qr, uh, ul, pieces):
    illums, waves = mine.shape[1:]
    spheres = uh.shape[1] // 2
    piece = jax.ShapeDtypeStruct((illums // pieces, 2 * MODES, spheres), F32)
    return pl.pallas_call(
        project_kernel,
        name="project",
        out_shape=(piece,) * pieces,
        in_specs=[VMEM] * 5,
        out_specs=(VMEM,) * pieces,
        scratch_shapes=[pltpu.VMEM((illums * MODES, 2 * waves), BF16)] * 2,
        compiler_params=PARAMS,
        cost_estimate=pl.CostEstimate(
            flops=6 * illums * MODES * 2 * waves * 2 * spheres,
            bytes_accessed=3 << 20,
            transcendentals=0,
        ),
    )(mine, other, qr, uh, ul)


def translate_kernel(
    pick_ref, slot_ref, base_ref, low_ref, own_ref, high_ref, inc_ref, idx_ref, class_ref, count_ref, trans_ref, out_ref, bh, bl, gh, gl
):
    own = pick_ref[0]
    slot = slot_ref[0]
    base = base_ref[0]
    spheres = own_ref.shape[2]
    local = idx_ref[...] - base
    side = jnp.right_shift(local, 7)
    lane = jnp.bitwise_and(local, 127)
    live = lax.broadcasted_iota(jnp.int32, local.shape, 0) < count_ref[...].reshape(1, spheres)
    kind = jnp.where(live, class_ref[...], OFFSETS)
    source = (low_ref[0], own_ref[0], high_ref[0])
    shape = (2 * MODES, spheres)
    picked = []
    for k in range(LINKS):
        at = jnp.broadcast_to(lane[k : k + 1, :], shape)
        got = [jnp.take_along_axis(x, at, axis=1) for x in source]
        pick = jnp.where(side[k : k + 1, :] == 0, got[0], got[2])
        picked.append(jnp.where(side[k : k + 1, :] == 1, got[1], pick))
    for c in range(OFFSETS):
        total = None
        for k in range(LINKS):
            term = jnp.where(kind[k : k + 1, :] == c, picked[k], 0.0)
            total = term if total is None else total + term
        hi, lo = split(total)
        rows = slice(c * MODES, (c + 1) * MODES)
        for ref, part in ((bh, hi), (bl, lo)):
            ref[rows, :spheres] = part[:MODES]
            ref[rows, spheres:] = part[MODES:]
        hi, lo = split(jnp.concatenate([trans_ref[0, c], trans_ref[1, c]], axis=0))
        gh[:, rows] = hi
        gl[:, rows] = lo
    both = dot3(gh[...], gl[...], bh[...], bl[...])
    upper, lower = both[:MODES], both[MODES:]
    result = jnp.concatenate(
        [upper[:, :spheres] - lower[:, spheres:], upper[:, spheres:] + lower[:, :spheres]], axis=0
    )
    result = result + inc_ref[own]
    out_ref[0] = jnp.where(slot == 0, result, 0.0)
    out_ref[1] = jnp.where(slot == 0, 0.0, result)


def translate(own, slot, base, low, mine, high, incident, index, link_class, link_count, translation):
    spheres = index.shape[1]
    return pl.pallas_call(
        translate_kernel,
        name="translate",
        out_shape=jax.ShapeDtypeStruct((2, 2 * MODES, spheres), F32),
        in_specs=[SMEM] * 3 + [VMEM] * 8,
        out_specs=VMEM,
        scratch_shapes=[
            pltpu.VMEM((OFFSETS * MODES, 2 * spheres), BF16),
            pltpu.VMEM((OFFSETS * MODES, 2 * spheres), BF16),
            pltpu.VMEM((2 * MODES, OFFSETS * MODES), BF16),
            pltpu.VMEM((2 * MODES, OFFSETS * MODES), BF16),
        ],
        compiler_params=PARAMS,
        cost_estimate=pl.CostEstimate(
            flops=6 * 2 * MODES * OFFSETS * MODES * 2 * spheres,
            bytes_accessed=2 << 20,
            transcendentals=0,
        ),
    )(own, slot, base, low, mine, high, incident, index, link_class, link_count, translation)


def types_kernel(mine_ref, other_ref, type_ref, th, tl, out_ref):
    count = mine_ref.shape[0]
    spheres = mine_ref.shape[2]
    kind = type_ref[...].reshape(1, spheres)
    for b in range(count):
        x = mine_ref[b] + other_ref[b]
        wide = jnp.concatenate([x[:MODES], x[MODES:]], axis=1)
        kinds = jnp.concatenate([kind, kind], axis=1)
        stacked = jnp.concatenate(
            [jnp.where(kinds == t, wide, 0.0) for t in range(TYPES)], axis=0
        )
        bh, bl = split(stacked)
        both = dot3(th[...], tl[...], bh, bl)
        upper, lower = both[:MODES], both[MODES:]
        out_ref[b, :MODES, :] = upper[:, :spheres] - lower[:, spheres:]
        out_ref[b, MODES:, :] = upper[:, spheres:] + lower[:, :spheres]


def apply_types(mine, other, sphere_type, th, tl):
    return pl.pallas_call(
        types_kernel,
        name="types",
        out_shape=jax.ShapeDtypeStruct(mine.shape, F32),
        in_specs=[VMEM] * 5,
        out_specs=VMEM,
        compiler_params=PARAMS,
        cost_estimate=pl.CostEstimate(
            flops=6 * 2 * MODES * TYPES * MODES * 4 * 128, bytes_accessed=1 << 20, transcendentals=0
        ),
    )(mine, other, sphere_type, th, tl)


def place_kernel(flip_ref, *refs):
    pieces, (out_ref, sems) = refs[:-2], refs[-2:]
    size = pieces[0].shape[0]
    copies = []
    for i, piece in enumerate(pieces):
        start = jnp.bitwise_xor(flip_ref[0], size * i)
        copies.append(pltpu.make_async_copy(piece, out_ref.at[pl.ds(start, size)], sems.at[i]))
    for copy in copies:
        copy.start()
    for copy in copies:
        copy.wait()


def place(flip, pieces):
    count = len(pieces)
    shape = (count * pieces[0].shape[0],) + pieces[0].shape[1:]
    return pl.pallas_call(
        place_kernel,
        name="place",
        out_shape=jax.ShapeDtypeStruct(shape, F32),
        in_specs=[SMEM] + [VMEM] * count,
        out_specs=HBM,
        scratch_shapes=[pltpu.SemaphoreType.DMA((count,))],
        compiler_params=PARAMS,
        cost_estimate=pl.CostEstimate(flops=0, bytes_accessed=1 << 20, transcendentals=0),
    )(flip, *pieces)


def swap(x, axis, mask):
    return lax.ppermute(x, axis, [(i, i ^ mask) for i in range(lax.axis_size(axis))])


def per_device(
    coefficients,
    incident,
    positions,
    neighbour_index,
    link_class,
    link_count,
    sphere_type,
    translation,
    t_matrix,
    wave_grid,
    vertical,
    expansion,
    reflection,
    projector,
):
    block = coefficients.shape[2]
    sph = lax.axis_index("sph")
    wave = lax.axis_index("wave")
    along_x = jnp.bitwise_and(wave, 3)
    slot = jnp.right_shift(wave, 2)
    own = 2 * along_x + slot
    flip = 2 * along_x

    part, mine = expand(
        flip[None], own[None], coefficients, positions, wave_grid, vertical, expansion
    )
    part = part + swap(part, "sph", 1)
    r6, r4, r2 = (swap(part, "sph", mask) for mask in (6, 4, 2))
    uh, ul, qr, th, tl = prepare(
        positions, wave_grid, vertical, reflection, projector, t_matrix
    )
    part = (part + r6) + (r2 + r4)
    other = swap(part, "sph", 12)
    count = lax.axis_size("sph")
    low = lax.ppermute(mine, "sph", [(i, i + 1) for i in range(count - 1)])
    high = lax.ppermute(mine, "sph", [(i + 1, i) for i in range(count - 1)])

    keep, to1, to2, to3 = project(part, other, qr, uh, ul, 4)
    got2, got1, got3 = (swap(x, "wave", mask) for x, mask in ((to2, 2), (to1, 1), (to3, 3)))
    translated = translate(
        own[None],
        slot[None],
        ((sph - 1) * block)[None],
        low,
        mine,
        high,
        incident,
        neighbour_index,
        link_class,
        link_count,
        translation,
    )
    summed = ((keep + translated) + got1) + (got2 + got3)
    across = swap(summed, "wave", 4)
    updated = apply_types(summed, across, sphere_type, th, tl)
    from2, from1, from3 = (swap(updated, "wave", mask) for mask in (2, 1, 3))
    return place(flip[None], (updated, from1, from2, from3))


def solution(mesh):
    placed = (
        P(None, None, "sph"),
        P(None, None, "sph"),
        P(None, "sph"),
        P(None, "sph"),
        P(None, "sph"),
        P("sph"),
        P("sph"),
        P(),
        P(),
        P(None, "wave"),
        P("wave"),
        P(None, None, None, "wave"),
        P(None, None, None, "wave"),
        P(None, None, None, "wave"),
    )

    return jax.shard_map(
        per_device, mesh=mesh, in_specs=placed, out_specs=P(None, None, "sph"), check_vma=False
    )
```

```python
import jax
import jax.numpy as jnp
from jax import lax
from jax.experimental import pallas as pl
from jax.experimental.pallas import tpu as pltpu
from jax.sharding import PartitionSpec as P


MODES = 48
OFFSETS = 26
TYPES = 4
LINKS = 12
INV_TWO_PI = 0.15915494309189535

SIN_POLY = (3.14159264, -5.16771008, 2.55007752, -0.59829129, 0.07765766)
COS_POLY = (1.0, -4.93480214, 4.05870916, -1.335212, 0.23493731, -0.02439632)

VMEM = pl.BlockSpec(memory_space=pltpu.VMEM)
HBM = pl.BlockSpec(memory_space=pltpu.HBM)
SMEM = pl.BlockSpec(memory_space=pltpu.SMEM)
BF16 = jnp.bfloat16
F32 = jnp.float32
PARAMS = pltpu.CompilerParams(vmem_limit_bytes=12 << 20)


def horner(coefs, t):
    acc = coefs[-1] * t + coefs[-2]
    for value in coefs[-3::-1]:
        acc = acc * t + value
    return acc


def cos_sin_turns(turns):
    rest = turns - jnp.round(turns)
    t = rest * rest
    s = rest * horner(SIN_POLY, t)
    c = horner(COS_POLY, t)
    return 1.0 - 2.0 * (s * s), 2.0 * (s * c)


def split(x):
    hi = x.astype(BF16)
    return hi, (x - hi.astype(F32)).astype(BF16)


def dot3(ah, al, bh, bl):
    def dot(a, b):
        return jnp.dot(a, b, preferred_element_type=F32)

    return dot(ah, bh) + (dot(ah, bl) + dot(al, bh))


def columns(rows):
    pad = jnp.zeros((8 - rows.shape[0], rows.shape[1]), F32)
    return jnp.concatenate([rows, pad], axis=0).T


def expand_kernel(
    flip_ref,
    own_ref,
    coef_hbm,
    pos_hbm,
    grid_hbm,
    vert_hbm,
    exp_hbm,
    out_ref,
    mine_ref,
    coef_ref,
    pos_ref,
    grid_ref,
    vert_ref,
    exp_ref,
    ah,
    al,
    spec,
    sems,
):
    illums = coef_ref.shape[0]
    flip = flip_ref[0]
    pairs = [(pos_hbm, pos_ref), (grid_hbm, grid_ref), (vert_hbm, vert_ref)]
    for b in range(illums):
        at = jnp.bitwise_xor(flip, b)
        pairs.append((coef_hbm.at[at], coef_ref.at[b]))
    for p in range(2):
        for i in range(2):
            pairs.append((exp_hbm.at[i, p], exp_ref.at[i, p]))
    copies = [
        pltpu.make_async_copy(source, target, sems.at[i]) for i, (source, target) in enumerate(pairs)
    ]
    for copy in copies:
        copy.start()
    waves = grid_ref.shape[1]
    half = illums * MODES
    for copy in copies[:3]:
        copy.wait()
    pos = columns(pos_ref[...])
    grid = grid_ref[...].astype(F32)
    vert = vert_ref[...].reshape(1, waves) * INV_TWO_PI
    turns = pos[:, 0:1] * grid[0:1] + pos[:, 1:2] * grid[1:2] - pos[:, 2:3] * vert
    cos, sin = cos_sin_turns(turns)
    bh, bl = split(jnp.concatenate([cos, sin], axis=0))
    for copy in copies[3 : 3 + illums]:
        copy.wait()
    mine = coef_ref[jnp.bitwise_xor(flip, own_ref[0])]
    mine_ref[0] = mine
    depth = mine.shape[0] * mine.shape[1] // waves
    for i in range(waves // mine.shape[1]):
        lanes = slice(i * mine.shape[1], (i + 1) * mine.shape[1])
        out_ref[4 * illums :, lanes] = mine[i * depth : (i + 1) * depth]
    for b in range(illums):
        block = coef_ref[b]
        re, im = block[:MODES], block[MODES:]
        for base, left, right in ((0, re, im), (half, im, -re)):
            rows = pl.ds(base + b * MODES, MODES)
            for offset, part in ((0, left), (128, right)):
                hi, lo = split(part)
                ah[rows, offset : offset + 128] = hi
                al[rows, offset : offset + 128] = lo
    for copy in copies[3 + illums :]:
        copy.wait()
    width = 256
    for start in range(0, waves, width):
        lanes = slice(start, start + width)
        spec[...] = dot3(ah[...], al[...], bh[:, lanes], bl[:, lanes])
        for p in range(2):
            er, ei = exp_ref[0, p, :, lanes], exp_ref[1, p, :, lanes]
            out_re, out_im = [], []
            for b in range(illums):
                sr = spec[b * MODES : (b + 1) * MODES, :]
                si = spec[half + b * MODES : half + (b + 1) * MODES, :]
                out_re.append(jnp.sum(er * sr - ei * si, axis=0, keepdims=True))
                out_im.append(jnp.sum(er * si + ei * sr, axis=0, keepdims=True))
            top = 2 * p * illums
            out_ref[top : top + illums, lanes] = jnp.concatenate(out_re, axis=0)
            out_ref[top + illums : top + 2 * illums, lanes] = jnp.concatenate(out_im, axis=0)


def expand(flip, own, coefficients, positions, wave_grid, vertical, expansion):
    illums, _, spheres = coefficients.shape
    waves = wave_grid.shape[1]
    rows = illums * 2 * MODES
    arrays = (coefficients, positions, wave_grid, vertical, expansion)
    return pl.pallas_call(
        expand_kernel,
        name="expand",
        out_shape=(
            jax.ShapeDtypeStruct((4 * illums + 2 * MODES * spheres // waves, waves), F32),
            jax.ShapeDtypeStruct((1, 2 * MODES, spheres), F32),
        ),
        in_specs=[SMEM] * 2 + [HBM] * 5,
        out_specs=(VMEM, VMEM),
        scratch_shapes=[pltpu.VMEM(x.shape, x.dtype) for x in arrays]
        + [
            pltpu.VMEM((rows, 2 * spheres), BF16),
            pltpu.VMEM((rows, 2 * spheres), BF16),
            pltpu.VMEM((rows, 256), F32),
            pltpu.SemaphoreType.DMA((7 + illums,)),
        ],
        compiler_params=PARAMS,
        cost_estimate=pl.CostEstimate(
            flops=6 * rows * 2 * spheres * waves, bytes_accessed=4 << 20, transcendentals=0
        ),
    )(flip, own, *(pltpu.with_memory_space_constraint(x, pltpu.HBM) for x in arrays))


def prepare_kernel(pos_ref, grid_ref, vert_ref, refl_ref, proj_ref, tmat_ref, uh, ul, qr_ref, th, tl):
    for t in range(TYPES):
        hi, lo = split(jnp.concatenate([tmat_ref[0, t], tmat_ref[1, t]], axis=0))
        th[:, t * MODES : (t + 1) * MODES] = hi
        tl[:, t * MODES : (t + 1) * MODES] = lo
    waves = grid_ref.shape[1]
    spheres = pos_ref.shape[1]
    grid = grid_ref[...].astype(F32)
    vert = vert_ref[...].reshape(1, waves) * INV_TWO_PI
    cols = columns(jnp.concatenate([grid, vert], axis=0))
    turns = cols[:, 0:1] * pos_ref[0:1, :] + cols[:, 1:2] * pos_ref[1:2, :]
    turns = turns + cols[:, 2:3] * pos_ref[2:3, :]
    cos, sin = cos_sin_turns(turns)
    ch, cl = split(cos)
    sh, sl = split(sin)
    for ref, c, s in ((uh, ch, sh), (ul, cl, sl)):
        ref[:waves, :spheres] = c
        ref[:waves, spheres:] = s
        ref[waves:, :spheres] = -s
        ref[waves:, spheres:] = c
    for q in range(2):
        acc_re = acc_im = None
        for p in range(2):
            pr, pi = proj_ref[0, :, p, :], proj_ref[1, :, p, :]
            rr = refl_ref[0, p, q : q + 1, :]
            ri = refl_ref[1, p, q : q + 1, :]
            term_re = pr * rr - pi * ri
            term_im = pr * ri + pi * rr
            acc_re = term_re if acc_re is None else acc_re + term_re
            acc_im = term_im if acc_im is None else acc_im + term_im
        qr_ref[2 * q] = acc_re
        qr_ref[2 * q + 1] = acc_im


def prepare(positions, wave_grid, vertical, reflection, projector, t_matrix):
    waves = wave_grid.shape[1]
    spheres = positions.shape[1]
    tiles = jax.ShapeDtypeStruct((2 * waves, 2 * spheres), BF16)
    types = jax.ShapeDtypeStruct((2 * MODES, TYPES * MODES), BF16)
    return pl.pallas_call(
        prepare_kernel,
        name="prepare",
        out_shape=(tiles, tiles, jax.ShapeDtypeStruct((4, MODES, waves), F32), types, types),
        in_specs=[VMEM] * 6,
        out_specs=(VMEM,) * 5,
        compiler_params=PARAMS,
        cost_estimate=pl.CostEstimate(
            flops=2 << 20, bytes_accessed=2 << 20, transcendentals=0
        ),
    )(positions, wave_grid, vertical, reflection, projector, t_matrix)


def project_kernel(mine_ref, other_ref, qr_ref, uh, ul, *refs):
    outs, (fh, fl) = refs[:-2], refs[-2:]
    illums = mine_ref.shape[1]
    waves = mine_ref.shape[2]
    width = 128
    for start in range(0, waves, width):
        lanes = slice(start, start + width)
        spec = [mine_ref[i, :, lanes] + other_ref[i, :, lanes] for i in range(4)]
        qr = [qr_ref[i, :, lanes] for i in range(4)]
        for b in range(illums):
            rows = slice(b * MODES, (b + 1) * MODES)
            x = [part[b : b + 1, :] for part in spec]
            fr = (qr[0] * x[0] - qr[1] * x[1]) + (qr[2] * x[2] - qr[3] * x[3])
            fi = (qr[0] * x[1] + qr[1] * x[0]) + (qr[2] * x[3] + qr[3] * x[2])
            for base, part in ((0, fr), (waves, fi)):
                hi, lo = split(part)
                fh[rows, base + start : base + start + width] = hi
                fl[rows, base + start : base + start + width] = lo
    out = dot3(fh[...], fl[...], uh[...], ul[...])
    per_piece = illums // len(outs)
    for b in range(illums):
        ref = outs[b // per_piece]
        rows = out[b * MODES : (b + 1) * MODES]
        ref[b % per_piece, :MODES, :] = rows[:, :128]
        ref[b % per_piece, MODES:, :] = rows[:, 128:]


def project(mine, other, qr, uh, ul, pieces):
    illums, waves = mine.shape[1:]
    spheres = uh.shape[1] // 2
    piece = jax.ShapeDtypeStruct((illums // pieces, 2 * MODES, spheres), F32)
    return pl.pallas_call(
        project_kernel,
        name="project",
        out_shape=(piece,) * pieces,
        in_specs=[VMEM] * 5,
        out_specs=(VMEM,) * pieces,
        scratch_shapes=[pltpu.VMEM((illums * MODES, 2 * waves), BF16)] * 2,
        compiler_params=PARAMS,
        cost_estimate=pl.CostEstimate(
            flops=6 * illums * MODES * 2 * waves * 2 * spheres,
            bytes_accessed=3 << 20,
            transcendentals=0,
        ),
    )(mine, other, qr, uh, ul)


def translate_kernel(
    pick_ref, slot_ref, base_ref, odd_ref, near_ref, own_ref, far_ref, inc_ref, idx_ref, class_ref, count_ref, trans_ref, out_ref, bh, bl, gh, gl
):
    own = pick_ref[0]
    slot = slot_ref[0]
    base = base_ref[0]
    spheres = own_ref.shape[2]
    local = idx_ref[...] - base
    side = jnp.right_shift(local, 7)
    lane = jnp.bitwise_and(local, 127)
    live = lax.broadcasted_iota(jnp.int32, local.shape, 0) < count_ref[...].reshape(1, spheres)
    kind = jnp.where(live, class_ref[...], OFFSETS)
    shape = (2 * MODES, spheres)
    blocks = near_ref.shape[1] // spheres
    depth = shape[0] // blocks
    rows = slice(near_ref.shape[0] - depth, near_ref.shape[0])
    near = jnp.concatenate(
        [near_ref[rows, i * spheres : (i + 1) * spheres] for i in range(blocks)], axis=0
    )
    far = far_ref[0]
    odd = odd_ref[0] == 1
    source = (jnp.where(odd, near, far), own_ref[0], jnp.where(odd, far, near))
    picked = []
    for k in range(LINKS):
        at = jnp.broadcast_to(lane[k : k + 1, :], shape)
        got = [jnp.take_along_axis(x, at, axis=1) for x in source]
        pick = jnp.where(side[k : k + 1, :] == 0, got[0], got[2])
        picked.append(jnp.where(side[k : k + 1, :] == 1, got[1], pick))
    for c in range(OFFSETS):
        total = None
        for k in range(LINKS):
            term = jnp.where(kind[k : k + 1, :] == c, picked[k], 0.0)
            total = term if total is None else total + term
        hi, lo = split(total)
        rows = slice(c * MODES, (c + 1) * MODES)
        for ref, part in ((bh, hi), (bl, lo)):
            ref[rows, :spheres] = part[:MODES]
            ref[rows, spheres:] = part[MODES:]
        hi, lo = split(jnp.concatenate([trans_ref[0, c], trans_ref[1, c]], axis=0))
        gh[:, rows] = hi
        gl[:, rows] = lo
    both = dot3(gh[...], gl[...], bh[...], bl[...])
    upper, lower = both[:MODES], both[MODES:]
    result = jnp.concatenate(
        [upper[:, :spheres] - lower[:, spheres:], upper[:, spheres:] + lower[:, :spheres]], axis=0
    )
    result = result + inc_ref[own]
    out_ref[0] = jnp.where(slot == 0, result, 0.0)
    out_ref[1] = jnp.where(slot == 0, 0.0, result)


def translate(own, slot, base, odd, near, mine, far, incident, index, link_class, link_count, translation):
    spheres = index.shape[1]
    return pl.pallas_call(
        translate_kernel,
        name="translate",
        out_shape=jax.ShapeDtypeStruct((2, 2 * MODES, spheres), F32),
        in_specs=[SMEM] * 4 + [VMEM] * 8,
        out_specs=VMEM,
        scratch_shapes=[
            pltpu.VMEM((OFFSETS * MODES, 2 * spheres), BF16),
            pltpu.VMEM((OFFSETS * MODES, 2 * spheres), BF16),
            pltpu.VMEM((2 * MODES, OFFSETS * MODES), BF16),
            pltpu.VMEM((2 * MODES, OFFSETS * MODES), BF16),
        ],
        compiler_params=PARAMS,
        cost_estimate=pl.CostEstimate(
            flops=6 * 2 * MODES * OFFSETS * MODES * 2 * spheres,
            bytes_accessed=2 << 20,
            transcendentals=0,
        ),
    )(own, slot, base, odd, near, mine, far, incident, index, link_class, link_count, translation)


def types_kernel(mine_ref, other_ref, type_ref, th, tl, out_ref):
    count = mine_ref.shape[0]
    spheres = mine_ref.shape[2]
    kind = type_ref[...].reshape(1, spheres)
    for b in range(count):
        x = mine_ref[b] + other_ref[b]
        wide = jnp.concatenate([x[:MODES], x[MODES:]], axis=1)
        kinds = jnp.concatenate([kind, kind], axis=1)
        stacked = jnp.concatenate(
            [jnp.where(kinds == t, wide, 0.0) for t in range(TYPES)], axis=0
        )
        bh, bl = split(stacked)
        both = dot3(th[...], tl[...], bh, bl)
        upper, lower = both[:MODES], both[MODES:]
        out_ref[b, :MODES, :] = upper[:, :spheres] - lower[:, spheres:]
        out_ref[b, MODES:, :] = upper[:, spheres:] + lower[:, :spheres]


def apply_types(mine, other, sphere_type, th, tl):
    return pl.pallas_call(
        types_kernel,
        name="types",
        out_shape=jax.ShapeDtypeStruct(mine.shape, F32),
        in_specs=[VMEM] * 5,
        out_specs=VMEM,
        compiler_params=PARAMS,
        cost_estimate=pl.CostEstimate(
            flops=6 * 2 * MODES * TYPES * MODES * 4 * 128, bytes_accessed=1 << 20, transcendentals=0
        ),
    )(mine, other, sphere_type, th, tl)


def place_kernel(flip_ref, *refs):
    pieces, (out_ref, sems) = refs[:-2], refs[-2:]
    size = pieces[0].shape[0]
    copies = []
    for i, piece in enumerate(pieces):
        start = jnp.bitwise_xor(flip_ref[0], size * i)
        copies.append(pltpu.make_async_copy(piece, out_ref.at[pl.ds(start, size)], sems.at[i]))
    for copy in copies:
        copy.start()
    for copy in copies:
        copy.wait()


def place(flip, pieces):
    count = len(pieces)
    shape = (count * pieces[0].shape[0],) + pieces[0].shape[1:]
    return pl.pallas_call(
        place_kernel,
        name="place",
        out_shape=jax.ShapeDtypeStruct(shape, F32),
        in_specs=[SMEM] + [VMEM] * count,
        out_specs=HBM,
        scratch_shapes=[pltpu.SemaphoreType.DMA((count,))],
        compiler_params=PARAMS,
        cost_estimate=pl.CostEstimate(flops=0, bytes_accessed=1 << 20, transcendentals=0),
    )(flip, *pieces)


def swap(x, axis, mask):
    return lax.ppermute(x, axis, [(i, i ^ mask) for i in range(lax.axis_size(axis))])


def per_device(
    coefficients,
    incident,
    positions,
    neighbour_index,
    link_class,
    link_count,
    sphere_type,
    translation,
    t_matrix,
    wave_grid,
    vertical,
    expansion,
    reflection,
    projector,
):
    block = coefficients.shape[2]
    sph = lax.axis_index("sph")
    wave = lax.axis_index("wave")
    along_x = jnp.bitwise_and(wave, 3)
    slot = jnp.right_shift(wave, 2)
    own = 2 * along_x + slot
    flip = 2 * along_x

    wide, mine = expand(
        flip[None], own[None], coefficients, positions, wave_grid, vertical, expansion
    )
    near = swap(wide, "sph", 1)
    rows = 4 * coefficients.shape[0]
    part = (wide[:rows] + near[:rows]).reshape(4, -1, wide.shape[1])
    r6, r4, r2 = (swap(part, "sph", mask) for mask in (6, 4, 2))
    uh, ul, qr, th, tl = prepare(
        positions, wave_grid, vertical, reflection, projector, t_matrix
    )
    part = (part + r6) + (r2 + r4)
    other = swap(part, "sph", 12)
    size = lax.axis_size("sph")
    links = [(i, (i + 1) % size) for i in range(1, size, 2)]
    far = lax.ppermute(mine, "sph", links + [(j, i) for i, j in links])

    keep, to1, to2, to3 = project(part, other, qr, uh, ul, 4)
    got2, got1, got3 = (swap(x, "wave", mask) for x, mask in ((to2, 2), (to1, 1), (to3, 3)))
    translated = translate(
        own[None],
        slot[None],
        ((sph - 1) * block)[None],
        jnp.bitwise_and(sph, 1)[None],
        near,
        mine,
        far,
        incident,
        neighbour_index,
        link_class,
        link_count,
        translation,
    )
    summed = ((keep + translated) + got1) + (got2 + got3)
    across = swap(summed, "wave", 4)
    updated = apply_types(summed, across, sphere_type, th, tl)
    from2, from1, from3 = (swap(updated, "wave", mask) for mask in (2, 1, 3))
    return place(flip[None], (updated, from1, from2, from3))


def solution(mesh):
    placed = (
        P(None, None, "sph"),
        P(None, None, "sph"),
        P(None, "sph"),
        P(None, "sph"),
        P(None, "sph"),
        P("sph"),
        P("sph"),
        P(),
        P(),
        P(None, "wave"),
        P("wave"),
        P(None, None, None, "wave"),
        P(None, None, None, "wave"),
        P(None, None, None, "wave"),
    )

    return jax.shard_map(
        per_device, mesh=mesh, in_specs=placed, out_specs=P(None, None, "sph"), check_vma=False
    )
```

```python
import jax
import jax.numpy as jnp
from jax import lax
from jax.experimental import pallas as pl
from jax.experimental.pallas import tpu as pltpu
from jax.sharding import PartitionSpec as P


MODES = 48
OFFSETS = 26
TYPES = 4
LINKS = 12
INV_TWO_PI = 0.15915494309189535

SIN_POLY = (3.14159264, -5.16771008, 2.55007752, -0.59829129, 0.07765766)
COS_POLY = (1.0, -4.93480214, 4.05870916, -1.335212, 0.23493731, -0.02439632)

VMEM = pl.BlockSpec(memory_space=pltpu.VMEM)
HBM = pl.BlockSpec(memory_space=pltpu.HBM)
SMEM = pl.BlockSpec(memory_space=pltpu.SMEM)
BF16 = jnp.bfloat16
F32 = jnp.float32
PARAMS = pltpu.CompilerParams(vmem_limit_bytes=12 << 20)


def horner(coefs, t):
    acc = coefs[-1] * t + coefs[-2]
    for value in coefs[-3::-1]:
        acc = acc * t + value
    return acc


def cos_sin_turns(turns):
    rest = turns - jnp.round(turns)
    t = rest * rest
    s = rest * horner(SIN_POLY, t)
    c = horner(COS_POLY, t)
    return 1.0 - 2.0 * (s * s), 2.0 * (s * c)


def split(x):
    hi = x.astype(BF16)
    return hi, (x - hi.astype(F32)).astype(BF16)


def dot3(ah, al, bh, bl):
    def dot(a, b):
        return jnp.dot(a, b, preferred_element_type=F32)

    return dot(ah, bh) + (dot(ah, bl) + dot(al, bh))


def columns(rows):
    pad = jnp.zeros((8 - rows.shape[0], rows.shape[1]), F32)
    return jnp.concatenate([rows, pad], axis=0).T


def expand_kernel(
    flip_ref,
    own_ref,
    coef_hbm,
    pos_hbm,
    grid_hbm,
    vert_hbm,
    exp_hbm,
    out_ref,
    mine_ref,
    coef_ref,
    pos_ref,
    grid_ref,
    vert_ref,
    exp_ref,
    ah,
    al,
    spec,
    sems,
):
    illums = coef_ref.shape[0]
    flip = flip_ref[0]
    pairs = [(pos_hbm, pos_ref), (grid_hbm, grid_ref), (vert_hbm, vert_ref)]
    for b in range(illums):
        at = jnp.bitwise_xor(flip, b)
        pairs.append((coef_hbm.at[at], coef_ref.at[b]))
    for p in range(2):
        for i in range(2):
            pairs.append((exp_hbm.at[i, p], exp_ref.at[i, p]))
    copies = [
        pltpu.make_async_copy(source, target, sems.at[i]) for i, (source, target) in enumerate(pairs)
    ]
    for copy in copies:
        copy.start()
    waves = grid_ref.shape[1]
    half = illums * MODES
    for copy in copies[:3]:
        copy.wait()
    pos = columns(pos_ref[...])
    grid = grid_ref[...].astype(F32)
    vert = vert_ref[...].reshape(1, waves) * INV_TWO_PI
    turns = pos[:, 0:1] * grid[0:1] + pos[:, 1:2] * grid[1:2] - pos[:, 2:3] * vert
    cos, sin = cos_sin_turns(turns)
    bh, bl = split(jnp.concatenate([cos, sin], axis=0))
    for copy in copies[3 : 3 + illums]:
        copy.wait()
    mine = coef_ref[jnp.bitwise_xor(flip, own_ref[0])]
    mine_ref[0] = mine
    depth = mine.shape[0] * mine.shape[1] // waves
    for i in range(waves // mine.shape[1]):
        lanes = slice(i * mine.shape[1], (i + 1) * mine.shape[1])
        out_ref[4 * illums :, lanes] = mine[i * depth : (i + 1) * depth]
    for b in range(illums):
        block = coef_ref[b]
        re, im = block[:MODES], block[MODES:]
        for base, left, right in ((0, re, im), (half, im, -re)):
            rows = pl.ds(base + b * MODES, MODES)
            for offset, part in ((0, left), (128, right)):
                hi, lo = split(part)
                ah[rows, offset : offset + 128] = hi
                al[rows, offset : offset + 128] = lo
    for copy in copies[3 + illums :]:
        copy.wait()
    width = 256
    for start in range(0, waves, width):
        lanes = slice(start, start + width)
        spec[...] = dot3(ah[...], al[...], bh[:, lanes], bl[:, lanes])
        for p in range(2):
            er, ei = exp_ref[0, p, :, lanes], exp_ref[1, p, :, lanes]
            out_re, out_im = [], []
            for b in range(illums):
                sr = spec[b * MODES : (b + 1) * MODES, :]
                si = spec[half + b * MODES : half + (b + 1) * MODES, :]
                out_re.append(jnp.sum(er * sr - ei * si, axis=0, keepdims=True))
                out_im.append(jnp.sum(er * si + ei * sr, axis=0, keepdims=True))
            top = 2 * p * illums
            out_ref[top : top + illums, lanes] = jnp.concatenate(out_re, axis=0)
            out_ref[top + illums : top + 2 * illums, lanes] = jnp.concatenate(out_im, axis=0)


def expand(flip, own, coefficients, positions, wave_grid, vertical, expansion):
    illums, _, spheres = coefficients.shape
    waves = wave_grid.shape[1]
    rows = illums * 2 * MODES
    arrays = (coefficients, positions, wave_grid, vertical, expansion)
    return pl.pallas_call(
        expand_kernel,
        name="expand",
        out_shape=(
            jax.ShapeDtypeStruct((4 * illums + 2 * MODES * spheres // waves, waves), F32),
            jax.ShapeDtypeStruct((1, 2 * MODES, spheres), F32),
        ),
        in_specs=[SMEM] * 2 + [HBM] * 5,
        out_specs=(VMEM, VMEM),
        scratch_shapes=[pltpu.VMEM(x.shape, x.dtype) for x in arrays]
        + [
            pltpu.VMEM((rows, 2 * spheres), BF16),
            pltpu.VMEM((rows, 2 * spheres), BF16),
            pltpu.VMEM((rows, 256), F32),
            pltpu.SemaphoreType.DMA((7 + illums,)),
        ],
        compiler_params=PARAMS,
        cost_estimate=pl.CostEstimate(
            flops=6 * rows * 2 * spheres * waves, bytes_accessed=4 << 20, transcendentals=0
        ),
    )(flip, own, *(pltpu.with_memory_space_constraint(x, pltpu.HBM) for x in arrays))


def prepare_kernel(pos_ref, grid_ref, vert_ref, refl_ref, proj_ref, tmat_ref, uh, ul, qr_ref, th, tl):
    for t in range(TYPES):
        hi, lo = split(jnp.concatenate([tmat_ref[0, t], tmat_ref[1, t]], axis=0))
        th[:, t * MODES : (t + 1) * MODES] = hi
        tl[:, t * MODES : (t + 1) * MODES] = lo
    waves = grid_ref.shape[1]
    spheres = pos_ref.shape[1]
    grid = grid_ref[...].astype(F32)
    vert = vert_ref[...].reshape(1, waves) * INV_TWO_PI
    cols = columns(jnp.concatenate([grid, vert], axis=0))
    turns = cols[:, 0:1] * pos_ref[0:1, :] + cols[:, 1:2] * pos_ref[1:2, :]
    turns = turns + cols[:, 2:3] * pos_ref[2:3, :]
    cos, sin = cos_sin_turns(turns)
    ch, cl = split(cos)
    sh, sl = split(sin)
    for ref, c, s in ((uh, ch, sh), (ul, cl, sl)):
        ref[:waves, :spheres] = c
        ref[:waves, spheres:] = s
        ref[waves:, :spheres] = -s
        ref[waves:, spheres:] = c
    for q in range(2):
        acc_re = acc_im = None
        for p in range(2):
            pr, pi = proj_ref[0, :, p, :], proj_ref[1, :, p, :]
            rr = refl_ref[0, p, q : q + 1, :]
            ri = refl_ref[1, p, q : q + 1, :]
            term_re = pr * rr - pi * ri
            term_im = pr * ri + pi * rr
            acc_re = term_re if acc_re is None else acc_re + term_re
            acc_im = term_im if acc_im is None else acc_im + term_im
        qr_ref[2 * q] = acc_re
        qr_ref[2 * q + 1] = acc_im


def prepare(positions, wave_grid, vertical, reflection, projector, t_matrix):
    waves = wave_grid.shape[1]
    spheres = positions.shape[1]
    tiles = jax.ShapeDtypeStruct((2 * waves, 2 * spheres), BF16)
    types = jax.ShapeDtypeStruct((2 * MODES, TYPES * MODES), BF16)
    return pl.pallas_call(
        prepare_kernel,
        name="prepare",
        out_shape=(tiles, tiles, jax.ShapeDtypeStruct((4, MODES, waves), F32), types, types),
        in_specs=[VMEM] * 6,
        out_specs=(VMEM,) * 5,
        compiler_params=PARAMS,
        cost_estimate=pl.CostEstimate(
            flops=2 << 20, bytes_accessed=2 << 20, transcendentals=0
        ),
    )(positions, wave_grid, vertical, reflection, projector, t_matrix)


def project_kernel(mine_ref, other_ref, qr_ref, uh, ul, *refs):
    outs, (fh, fl) = refs[:-2], refs[-2:]
    illums = mine_ref.shape[1]
    waves = mine_ref.shape[2]
    width = 128
    for start in range(0, waves, width):
        lanes = slice(start, start + width)
        spec = [mine_ref[i, :, lanes] + other_ref[i, :, lanes] for i in range(4)]
        qr = [qr_ref[i, :, lanes] for i in range(4)]
        for b in range(illums):
            rows = slice(b * MODES, (b + 1) * MODES)
            x = [part[b : b + 1, :] for part in spec]
            fr = (qr[0] * x[0] - qr[1] * x[1]) + (qr[2] * x[2] - qr[3] * x[3])
            fi = (qr[0] * x[1] + qr[1] * x[0]) + (qr[2] * x[3] + qr[3] * x[2])
            for base, part in ((0, fr), (waves, fi)):
                hi, lo = split(part)
                fh[rows, base + start : base + start + width] = hi
                fl[rows, base + start : base + start + width] = lo
    out = dot3(fh[...], fl[...], uh[...], ul[...])
    per_piece = illums // len(outs)
    for b in range(illums):
        ref = outs[b // per_piece]
        rows = out[b * MODES : (b + 1) * MODES]
        ref[b % per_piece, :MODES, :] = rows[:, :128]
        ref[b % per_piece, MODES:, :] = rows[:, 128:]


def project(mine, other, qr, uh, ul, pieces):
    illums, waves = mine.shape[1:]
    spheres = uh.shape[1] // 2
    piece = jax.ShapeDtypeStruct((illums // pieces, 2 * MODES, spheres), F32)
    return pl.pallas_call(
        project_kernel,
        name="project",
        out_shape=(piece,) * pieces,
        in_specs=[VMEM] * 5,
        out_specs=(VMEM,) * pieces,
        scratch_shapes=[pltpu.VMEM((illums * MODES, 2 * waves), BF16)] * 2,
        compiler_params=PARAMS,
        cost_estimate=pl.CostEstimate(
            flops=6 * illums * MODES * 2 * waves * 2 * spheres,
            bytes_accessed=3 << 20,
            transcendentals=0,
        ),
    )(mine, other, qr, uh, ul)


def translate_kernel(
    pick_ref, slot_ref, base_ref, odd_ref, near_ref, own_ref, far_ref, inc_ref, idx_ref, class_ref, count_ref, trans_ref, out_ref, bh, bl, gh, gl
):
    own = pick_ref[0]
    slot = slot_ref[0]
    base = base_ref[0]
    spheres = own_ref.shape[2]
    local = idx_ref[...] - base
    side = jnp.right_shift(local, 7)
    lane = jnp.bitwise_and(local, 127)
    live = lax.broadcasted_iota(jnp.int32, local.shape, 0) < count_ref[...].reshape(1, spheres)
    kind = jnp.where(live, class_ref[...], OFFSETS)
    shape = (2 * MODES, spheres)
    blocks = near_ref.shape[1] // spheres
    depth = shape[0] // blocks
    rows = slice(near_ref.shape[0] - depth, near_ref.shape[0])
    near = jnp.concatenate(
        [near_ref[rows, i * spheres : (i + 1) * spheres] for i in range(blocks)], axis=0
    )
    far = far_ref[0]
    odd = odd_ref[0] == 1
    source = (jnp.where(odd, near, far), own_ref[0], jnp.where(odd, far, near))
    picked = []
    for k in range(LINKS):
        at = jnp.broadcast_to(lane[k : k + 1, :], shape)
        got = [jnp.take_along_axis(x, at, axis=1) for x in source]
        pick = jnp.where(side[k : k + 1, :] == 0, got[0], got[2])
        picked.append(jnp.where(side[k : k + 1, :] == 1, got[1], pick))
    for c in range(OFFSETS):
        total = None
        for k in range(LINKS):
            term = jnp.where(kind[k : k + 1, :] == c, picked[k], 0.0)
            total = term if total is None else total + term
        hi, lo = split(total)
        rows = slice(c * MODES, (c + 1) * MODES)
        for ref, part in ((bh, hi), (bl, lo)):
            ref[rows, :spheres] = part[:MODES]
            ref[rows, spheres:] = part[MODES:]
        hi, lo = split(jnp.concatenate([trans_ref[0, c], trans_ref[1, c]], axis=0))
        gh[:, rows] = hi
        gl[:, rows] = lo
    both = dot3(gh[...], gl[...], bh[...], bl[...])
    upper, lower = both[:MODES], both[MODES:]
    result = jnp.concatenate(
        [upper[:, :spheres] - lower[:, spheres:], upper[:, spheres:] + lower[:, :spheres]], axis=0
    )
    result = result + inc_ref[own]
    out_ref[0] = jnp.where(slot == 0, result, 0.0)
    out_ref[1] = jnp.where(slot == 0, 0.0, result)


def translate(own, slot, base, odd, near, mine, far, incident, index, link_class, link_count, translation):
    spheres = index.shape[1]
    return pl.pallas_call(
        translate_kernel,
        name="translate",
        out_shape=jax.ShapeDtypeStruct((2, 2 * MODES, spheres), F32),
        in_specs=[SMEM] * 4 + [VMEM] * 8,
        out_specs=VMEM,
        scratch_shapes=[
            pltpu.VMEM((OFFSETS * MODES, 2 * spheres), BF16),
            pltpu.VMEM((OFFSETS * MODES, 2 * spheres), BF16),
            pltpu.VMEM((2 * MODES, OFFSETS * MODES), BF16),
            pltpu.VMEM((2 * MODES, OFFSETS * MODES), BF16),
        ],
        compiler_params=PARAMS,
        cost_estimate=pl.CostEstimate(
            flops=6 * 2 * MODES * OFFSETS * MODES * 2 * spheres,
            bytes_accessed=2 << 20,
            transcendentals=0,
        ),
    )(own, slot, base, odd, near, mine, far, incident, index, link_class, link_count, translation)


def types_kernel(mine_ref, other_ref, type_ref, th, tl, out_ref):
    count = mine_ref.shape[0]
    spheres = mine_ref.shape[2]
    kind = type_ref[...].reshape(1, spheres)
    for b in range(count):
        x = mine_ref[b] + other_ref[b]
        wide = jnp.concatenate([x[:MODES], x[MODES:]], axis=1)
        kinds = jnp.concatenate([kind, kind], axis=1)
        stacked = jnp.concatenate(
            [jnp.where(kinds == t, wide, 0.0) for t in range(TYPES)], axis=0
        )
        bh, bl = split(stacked)
        both = dot3(th[...], tl[...], bh, bl)
        upper, lower = both[:MODES], both[MODES:]
        out_ref[b, :MODES, :] = upper[:, :spheres] - lower[:, spheres:]
        out_ref[b, MODES:, :] = upper[:, spheres:] + lower[:, :spheres]


def apply_types(mine, other, sphere_type, th, tl):
    return pl.pallas_call(
        types_kernel,
        name="types",
        out_shape=jax.ShapeDtypeStruct(mine.shape, F32),
        in_specs=[VMEM] * 5,
        out_specs=VMEM,
        compiler_params=PARAMS,
        cost_estimate=pl.CostEstimate(
            flops=6 * 2 * MODES * TYPES * MODES * 4 * 128, bytes_accessed=1 << 20, transcendentals=0
        ),
    )(mine, other, sphere_type, th, tl)


def place_kernel(flip_ref, *refs):
    pieces, (out_ref, sems) = refs[:-2], refs[-2:]
    size = pieces[0].shape[0]
    copies = []
    for i, piece in enumerate(pieces):
        start = jnp.bitwise_xor(flip_ref[0], size * i)
        copies.append(pltpu.make_async_copy(piece, out_ref.at[pl.ds(start, size)], sems.at[i]))
    for copy in copies:
        copy.start()
    for copy in copies:
        copy.wait()


def place(flip, pieces):
    count = len(pieces)
    shape = (count * pieces[0].shape[0],) + pieces[0].shape[1:]
    return pl.pallas_call(
        place_kernel,
        name="place",
        out_shape=jax.ShapeDtypeStruct(shape, F32),
        in_specs=[SMEM] + [VMEM] * count,
        out_specs=HBM,
        scratch_shapes=[pltpu.SemaphoreType.DMA((count,))],
        compiler_params=PARAMS,
        cost_estimate=pl.CostEstimate(flops=0, bytes_accessed=1 << 20, transcendentals=0),
    )(flip, *pieces)


def swap(x, axis, mask):
    return lax.ppermute(x, axis, [(i, i ^ mask) for i in range(lax.axis_size(axis))])


def peers(x, axis, masks):
    pairs = [(i, i ^ masks[i & 1]) for i in range(lax.axis_size(axis))]
    return lax.ppermute(x, axis, pairs)


def per_device(
    coefficients,
    incident,
    positions,
    neighbour_index,
    link_class,
    link_count,
    sphere_type,
    translation,
    t_matrix,
    wave_grid,
    vertical,
    expansion,
    reflection,
    projector,
):
    block = coefficients.shape[2]
    sph = lax.axis_index("sph")
    wave = lax.axis_index("wave")
    along_x = jnp.bitwise_and(wave, 3)
    slot = jnp.right_shift(wave, 2)
    own = 2 * along_x + slot
    flip = 2 * along_x

    wide, mine = expand(
        flip[None], own[None], coefficients, positions, wave_grid, vertical, expansion
    )
    near = swap(wide, "sph", 1)
    rows = 4 * coefficients.shape[0]
    part = (wide[:rows] + near[:rows]).reshape(4, -1, wide.shape[1])
    even = jnp.bitwise_and(sph, 1) == 0
    r6, r4, r2, r1 = (
        peers(part, "sph", masks)
        for masks in ((10, 14), (12, 8), (4, 6), (4, 2))
    )
    uh, ul, qr, th, tl = prepare(
        positions, wave_grid, vertical, reflection, projector, t_matrix
    )
    part = (jnp.where(even, part, r1) + r6) + (r2 + r4)
    other = swap(part, "sph", 1)
    size = lax.axis_size("sph")
    links = [(i, (i + 1) % size) for i in range(1, size, 2)]
    far = lax.ppermute(mine, "sph", links + [(j, i) for i, j in links])

    keep, to1, to2, to3 = project(part, other, qr, uh, ul, 4)
    got2, got1, got3 = (swap(x, "wave", mask) for x, mask in ((to2, 2), (to1, 1), (to3, 3)))
    translated = translate(
        own[None],
        slot[None],
        ((sph - 1) * block)[None],
        jnp.bitwise_and(sph, 1)[None],
        near,
        mine,
        far,
        incident,
        neighbour_index,
        link_class,
        link_count,
        translation,
    )
    summed = ((keep + translated) + got1) + (got2 + got3)
    across = swap(summed, "wave", 4)
    updated = apply_types(summed, across, sphere_type, th, tl)
    from2, from1, from3 = (swap(updated, "wave", mask) for mask in (2, 1, 3))
    return place(flip[None], (updated, from1, from2, from3))


def solution(mesh):
    placed = (
        P(None, None, "sph"),
        P(None, None, "sph"),
        P(None, "sph"),
        P(None, "sph"),
        P(None, "sph"),
        P("sph"),
        P("sph"),
        P(),
        P(),
        P(None, "wave"),
        P("wave"),
        P(None, None, None, "wave"),
        P(None, None, None, "wave"),
        P(None, None, None, "wave"),
    )

    return jax.shard_map(
        per_device, mesh=mesh, in_specs=placed, out_specs=P(None, None, "sph"), check_vma=False
    )
```

```python
import jax
import jax.numpy as jnp
from jax import lax
from jax.experimental import pallas as pl
from jax.experimental.pallas import tpu as pltpu
from jax.sharding import PartitionSpec as P


MODES = 48
OFFSETS = 26
TYPES = 4
LINKS = 12
INV_TWO_PI = 0.15915494309189535

SIN_POLY = (3.14159264, -5.16771008, 2.55007752, -0.59829129, 0.07765766)
COS_POLY = (1.0, -4.93480214, 4.05870916, -1.335212, 0.23493731, -0.02439632)

VMEM = pl.BlockSpec(memory_space=pltpu.VMEM)
HBM = pl.BlockSpec(memory_space=pltpu.HBM)
SMEM = pl.BlockSpec(memory_space=pltpu.SMEM)
BF16 = jnp.bfloat16
F32 = jnp.float32
PARAMS = pltpu.CompilerParams(vmem_limit_bytes=12 << 20)


def horner(coefs, t):
    acc = coefs[-1] * t + coefs[-2]
    for value in coefs[-3::-1]:
        acc = acc * t + value
    return acc


def cos_sin_turns(turns):
    rest = turns - jnp.round(turns)
    t = rest * rest
    s = rest * horner(SIN_POLY, t)
    c = horner(COS_POLY, t)
    return 1.0 - 2.0 * (s * s), 2.0 * (s * c)


def split(x):
    hi = x.astype(BF16)
    return hi, (x - hi.astype(F32)).astype(BF16)


def dot3(ah, al, bh, bl):
    def dot(a, b):
        return jnp.dot(a, b, preferred_element_type=F32)

    return dot(jnp.concatenate([ah, ah, al], axis=1), jnp.concatenate([bh, bl, bh], axis=0))


def columns(rows):
    pad = jnp.zeros((8 - rows.shape[0], rows.shape[1]), F32)
    return jnp.concatenate([rows, pad], axis=0).T


def expand_kernel(
    flip_ref,
    own_ref,
    coef_hbm,
    pos_hbm,
    grid_hbm,
    vert_hbm,
    exp_hbm,
    out_ref,
    mine_ref,
    coef_ref,
    pos_ref,
    grid_ref,
    vert_ref,
    exp_ref,
    ah,
    al,
    spec,
    sems,
):
    illums = coef_ref.shape[0]
    flip = flip_ref[0]
    pairs = [(pos_hbm, pos_ref), (grid_hbm, grid_ref), (vert_hbm, vert_ref)]
    for b in range(illums):
        at = jnp.bitwise_xor(flip, b)
        pairs.append((coef_hbm.at[at], coef_ref.at[b]))
    for p in range(2):
        for i in range(2):
            pairs.append((exp_hbm.at[i, p], exp_ref.at[i, p]))
    copies = [
        pltpu.make_async_copy(source, target, sems.at[i]) for i, (source, target) in enumerate(pairs)
    ]
    for copy in copies:
        copy.start()
    waves = grid_ref.shape[1]
    half = illums * MODES
    for copy in copies[:3]:
        copy.wait()
    pos = columns(pos_ref[...])
    grid = grid_ref[...].astype(F32)
    vert = vert_ref[...].reshape(1, waves) * INV_TWO_PI
    turns = pos[:, 0:1] * grid[0:1] + pos[:, 1:2] * grid[1:2] - pos[:, 2:3] * vert
    cos, sin = cos_sin_turns(turns)
    bh, bl = split(jnp.concatenate([cos, sin], axis=0))
    for copy in copies[3 : 3 + illums]:
        copy.wait()
    mine = coef_ref[jnp.bitwise_xor(flip, own_ref[0])]
    mine_ref[0] = mine
    depth = mine.shape[0] * mine.shape[1] // waves
    for i in range(waves // mine.shape[1]):
        lanes = slice(i * mine.shape[1], (i + 1) * mine.shape[1])
        out_ref[4 * illums :, lanes] = mine[i * depth : (i + 1) * depth]
    for b in range(illums):
        block = coef_ref[b]
        re, im = block[:MODES], block[MODES:]
        for base, left, right in ((0, re, im), (half, im, -re)):
            rows = pl.ds(base + b * MODES, MODES)
            for offset, part in ((0, left), (128, right)):
                hi, lo = split(part)
                ah[rows, offset : offset + 128] = hi
                al[rows, offset : offset + 128] = lo
    for copy in copies[3 + illums :]:
        copy.wait()
    width = 512
    for start in range(0, waves, width):
        lanes = slice(start, start + width)
        spec[...] = dot3(ah[...], al[...], bh[:, lanes], bl[:, lanes])
        for p in range(2):
            er, ei = exp_ref[0, p, :, lanes], exp_ref[1, p, :, lanes]
            out_re, out_im = [], []
            for b in range(illums):
                sr = spec[b * MODES : (b + 1) * MODES, :]
                si = spec[half + b * MODES : half + (b + 1) * MODES, :]
                out_re.append(jnp.sum(er * sr - ei * si, axis=0, keepdims=True))
                out_im.append(jnp.sum(er * si + ei * sr, axis=0, keepdims=True))
            top = 2 * p * illums
            out_ref[top : top + illums, lanes] = jnp.concatenate(out_re, axis=0)
            out_ref[top + illums : top + 2 * illums, lanes] = jnp.concatenate(out_im, axis=0)


def expand(flip, own, coefficients, positions, wave_grid, vertical, expansion):
    illums, _, spheres = coefficients.shape
    waves = wave_grid.shape[1]
    rows = illums * 2 * MODES
    arrays = (coefficients, positions, wave_grid, vertical, expansion)
    return pl.pallas_call(
        expand_kernel,
        name="expand",
        out_shape=(
            jax.ShapeDtypeStruct((4 * illums + 2 * MODES * spheres // waves, waves), F32),
            jax.ShapeDtypeStruct((1, 2 * MODES, spheres), F32),
        ),
        in_specs=[SMEM] * 2 + [HBM] * 5,
        out_specs=(VMEM, VMEM),
        scratch_shapes=[pltpu.VMEM(x.shape, x.dtype) for x in arrays]
        + [
            pltpu.VMEM((rows, 2 * spheres), BF16),
            pltpu.VMEM((rows, 2 * spheres), BF16),
            pltpu.VMEM((rows, 512), F32),
            pltpu.SemaphoreType.DMA((7 + illums,)),
        ],
        compiler_params=PARAMS,
        cost_estimate=pl.CostEstimate(
            flops=6 * rows * 2 * spheres * waves, bytes_accessed=4 << 20, transcendentals=0
        ),
    )(flip, own, *(pltpu.with_memory_space_constraint(x, pltpu.HBM) for x in arrays))


def prepare_kernel(pos_ref, grid_ref, vert_ref, refl_ref, proj_ref, tmat_ref, uh, ul, qr_ref, th, tl):
    for t in range(TYPES):
        hi, lo = split(jnp.concatenate([tmat_ref[0, t], tmat_ref[1, t]], axis=0))
        th[:, t * MODES : (t + 1) * MODES] = hi
        tl[:, t * MODES : (t + 1) * MODES] = lo
    waves = grid_ref.shape[1]
    spheres = pos_ref.shape[1]
    grid = grid_ref[...].astype(F32)
    vert = vert_ref[...].reshape(1, waves) * INV_TWO_PI
    cols = columns(jnp.concatenate([grid, vert], axis=0))
    turns = cols[:, 0:1] * pos_ref[0:1, :] + cols[:, 1:2] * pos_ref[1:2, :]
    turns = turns + cols[:, 2:3] * pos_ref[2:3, :]
    cos, sin = cos_sin_turns(turns)
    ch, cl = split(cos)
    sh, sl = split(sin)
    for ref, c, s in ((uh, ch, sh), (ul, cl, sl)):
        ref[:waves, :spheres] = c
        ref[:waves, spheres:] = s
        ref[waves:, :spheres] = -s
        ref[waves:, spheres:] = c
    for q in range(2):
        acc_re = acc_im = None
        for p in range(2):
            pr, pi = proj_ref[0, :, p, :], proj_ref[1, :, p, :]
            rr = refl_ref[0, p, q : q + 1, :]
            ri = refl_ref[1, p, q : q + 1, :]
            term_re = pr * rr - pi * ri
            term_im = pr * ri + pi * rr
            acc_re = term_re if acc_re is None else acc_re + term_re
            acc_im = term_im if acc_im is None else acc_im + term_im
        qr_ref[2 * q] = acc_re
        qr_ref[2 * q + 1] = acc_im


def prepare(positions, wave_grid, vertical, reflection, projector, t_matrix):
    waves = wave_grid.shape[1]
    spheres = positions.shape[1]
    tiles = jax.ShapeDtypeStruct((2 * waves, 2 * spheres), BF16)
    types = jax.ShapeDtypeStruct((2 * MODES, TYPES * MODES), BF16)
    return pl.pallas_call(
        prepare_kernel,
        name="prepare",
        out_shape=(tiles, tiles, jax.ShapeDtypeStruct((4, MODES, waves), F32), types, types),
        in_specs=[VMEM] * 6,
        out_specs=(VMEM,) * 5,
        compiler_params=PARAMS,
        cost_estimate=pl.CostEstimate(
            flops=2 << 20, bytes_accessed=2 << 20, transcendentals=0
        ),
    )(positions, wave_grid, vertical, reflection, projector, t_matrix)


def project_kernel(mine_ref, other_ref, qr_ref, uh, ul, *refs):
    outs, (fh, fl) = refs[:-2], refs[-2:]
    illums = mine_ref.shape[1]
    waves = mine_ref.shape[2]
    width = 128
    for start in range(0, waves, width):
        lanes = slice(start, start + width)
        spec = [mine_ref[i, :, lanes] + other_ref[i, :, lanes] for i in range(4)]
        qr = [qr_ref[i, :, lanes] for i in range(4)]
        for b in range(illums):
            rows = slice(b * MODES, (b + 1) * MODES)
            x = [part[b : b + 1, :] for part in spec]
            fr = (qr[0] * x[0] - qr[1] * x[1]) + (qr[2] * x[2] - qr[3] * x[3])
            fi = (qr[0] * x[1] + qr[1] * x[0]) + (qr[2] * x[3] + qr[3] * x[2])
            for base, part in ((0, fr), (waves, fi)):
                hi, lo = split(part)
                fh[rows, base + start : base + start + width] = hi
                fl[rows, base + start : base + start + width] = lo
    out = dot3(fh[...], fl[...], uh[...], ul[...])
    per_piece = illums // len(outs)
    for b in range(illums):
        ref = outs[b // per_piece]
        rows = out[b * MODES : (b + 1) * MODES]
        ref[b % per_piece, :MODES, :] = rows[:, :128]
        ref[b % per_piece, MODES:, :] = rows[:, 128:]


def project(mine, other, qr, uh, ul, pieces):
    illums, waves = mine.shape[1:]
    spheres = uh.shape[1] // 2
    piece = jax.ShapeDtypeStruct((illums // pieces, 2 * MODES, spheres), F32)
    return pl.pallas_call(
        project_kernel,
        name="project",
        out_shape=(piece,) * pieces,
        in_specs=[VMEM] * 5,
        out_specs=(VMEM,) * pieces,
        scratch_shapes=[pltpu.VMEM((illums * MODES, 2 * waves), BF16)] * 2,
        compiler_params=PARAMS,
        cost_estimate=pl.CostEstimate(
            flops=6 * illums * MODES * 2 * waves * 2 * spheres,
            bytes_accessed=3 << 20,
            transcendentals=0,
        ),
    )(mine, other, qr, uh, ul)


def translate_kernel(
    pick_ref, slot_ref, base_ref, odd_ref, near_ref, own_ref, far_ref, inc_ref, idx_ref, class_ref, count_ref, trans_ref, out_ref, bh, bl, gh, gl
):
    own = pick_ref[0]
    slot = slot_ref[0]
    base = base_ref[0]
    spheres = own_ref.shape[2]
    local = idx_ref[...] - base
    side = jnp.right_shift(local, 7)
    lane = jnp.bitwise_and(local, 127)
    live = lax.broadcasted_iota(jnp.int32, local.shape, 0) < count_ref[...].reshape(1, spheres)
    kind = jnp.where(live, class_ref[...], OFFSETS)
    shape = (2 * MODES, spheres)
    blocks = near_ref.shape[1] // spheres
    depth = shape[0] // blocks
    rows = slice(near_ref.shape[0] - depth, near_ref.shape[0])
    near = jnp.concatenate(
        [near_ref[rows, i * spheres : (i + 1) * spheres] for i in range(blocks)], axis=0
    )
    far = far_ref[0]
    odd = odd_ref[0] == 1
    source = (jnp.where(odd, near, far), own_ref[0], jnp.where(odd, far, near))
    picked = []
    for k in range(LINKS):
        at = jnp.broadcast_to(lane[k : k + 1, :], shape)
        got = [jnp.take_along_axis(x, at, axis=1) for x in source]
        pick = jnp.where(side[k : k + 1, :] == 0, got[0], got[2])
        picked.append(jnp.where(side[k : k + 1, :] == 1, got[1], pick))
    for c in range(OFFSETS):
        total = None
        for k in range(LINKS):
            term = jnp.where(kind[k : k + 1, :] == c, picked[k], 0.0)
            total = term if total is None else total + term
        hi, lo = split(total)
        rows = slice(c * MODES, (c + 1) * MODES)
        for ref, part in ((bh, hi), (bl, lo)):
            ref[rows, :spheres] = part[:MODES]
            ref[rows, spheres:] = part[MODES:]
        hi, lo = split(jnp.concatenate([trans_ref[0, c], trans_ref[1, c]], axis=0))
        gh[:, rows] = hi
        gl[:, rows] = lo
    both = dot3(gh[...], gl[...], bh[...], bl[...])
    upper, lower = both[:MODES], both[MODES:]
    result = jnp.concatenate(
        [upper[:, :spheres] - lower[:, spheres:], upper[:, spheres:] + lower[:, :spheres]], axis=0
    )
    result = result + inc_ref[own]
    out_ref[0] = jnp.where(slot == 0, result, 0.0)
    out_ref[1] = jnp.where(slot == 0, 0.0, result)


def translate(own, slot, base, odd, near, mine, far, incident, index, link_class, link_count, translation):
    spheres = index.shape[1]
    return pl.pallas_call(
        translate_kernel,
        name="translate",
        out_shape=jax.ShapeDtypeStruct((2, 2 * MODES, spheres), F32),
        in_specs=[SMEM] * 4 + [VMEM] * 8,
        out_specs=VMEM,
        scratch_shapes=[
            pltpu.VMEM((OFFSETS * MODES, 2 * spheres), BF16),
            pltpu.VMEM((OFFSETS * MODES, 2 * spheres), BF16),
            pltpu.VMEM((2 * MODES, OFFSETS * MODES), BF16),
            pltpu.VMEM((2 * MODES, OFFSETS * MODES), BF16),
        ],
        compiler_params=PARAMS,
        cost_estimate=pl.CostEstimate(
            flops=6 * 2 * MODES * OFFSETS * MODES * 2 * spheres,
            bytes_accessed=2 << 20,
            transcendentals=0,
        ),
    )(own, slot, base, odd, near, mine, far, incident, index, link_class, link_count, translation)


def types_kernel(mine_ref, other_ref, type_ref, th, tl, out_ref):
    count = mine_ref.shape[0]
    spheres = mine_ref.shape[2]
    kind = type_ref[...].reshape(1, spheres)
    for b in range(count):
        x = mine_ref[b] + other_ref[b]
        wide = jnp.concatenate([x[:MODES], x[MODES:]], axis=1)
        kinds = jnp.concatenate([kind, kind], axis=1)
        stacked = jnp.concatenate(
            [jnp.where(kinds == t, wide, 0.0) for t in range(TYPES)], axis=0
        )
        bh, bl = split(stacked)
        both = dot3(th[...], tl[...], bh, bl)
        upper, lower = both[:MODES], both[MODES:]
        out_ref[b, :MODES, :] = upper[:, :spheres] - lower[:, spheres:]
        out_ref[b, MODES:, :] = upper[:, spheres:] + lower[:, :spheres]


def apply_types(mine, other, sphere_type, th, tl):
    return pl.pallas_call(
        types_kernel,
        name="types",
        out_shape=jax.ShapeDtypeStruct(mine.shape, F32),
        in_specs=[VMEM] * 5,
        out_specs=VMEM,
        compiler_params=PARAMS,
        cost_estimate=pl.CostEstimate(
            flops=6 * 2 * MODES * TYPES * MODES * 4 * 128, bytes_accessed=1 << 20, transcendentals=0
        ),
    )(mine, other, sphere_type, th, tl)


def place_kernel(flip_ref, *refs):
    pieces, (out_ref, sems) = refs[:-2], refs[-2:]
    size = pieces[0].shape[0]
    copies = []
    for i, piece in enumerate(pieces):
        start = jnp.bitwise_xor(flip_ref[0], size * i)
        copies.append(pltpu.make_async_copy(piece, out_ref.at[pl.ds(start, size)], sems.at[i]))
    for copy in copies:
        copy.start()
    for copy in copies:
        copy.wait()


def place(flip, pieces):
    count = len(pieces)
    shape = (count * pieces[0].shape[0],) + pieces[0].shape[1:]
    return pl.pallas_call(
        place_kernel,
        name="place",
        out_shape=jax.ShapeDtypeStruct(shape, F32),
        in_specs=[SMEM] + [VMEM] * count,
        out_specs=HBM,
        scratch_shapes=[pltpu.SemaphoreType.DMA((count,))],
        compiler_params=PARAMS,
        cost_estimate=pl.CostEstimate(flops=0, bytes_accessed=1 << 20, transcendentals=0),
    )(flip, *pieces)


def swap(x, axis, mask):
    return lax.ppermute(x, axis, [(i, i ^ mask) for i in range(lax.axis_size(axis))])


def peers(x, axis, masks):
    pairs = [(i, i ^ masks[i & 1]) for i in range(lax.axis_size(axis))]
    return lax.ppermute(x, axis, pairs)


def per_device(
    coefficients,
    incident,
    positions,
    neighbour_index,
    link_class,
    link_count,
    sphere_type,
    translation,
    t_matrix,
    wave_grid,
    vertical,
    expansion,
    reflection,
    projector,
):
    block = coefficients.shape[2]
    sph = lax.axis_index("sph")
    wave = lax.axis_index("wave")
    along_x = jnp.bitwise_and(wave, 3)
    slot = jnp.right_shift(wave, 2)
    own = 2 * along_x + slot
    flip = 2 * along_x

    wide, mine = expand(
        flip[None], own[None], coefficients, positions, wave_grid, vertical, expansion
    )
    near = swap(wide, "sph", 1)
    rows = 4 * coefficients.shape[0]
    part = (wide[:rows] + near[:rows]).reshape(4, -1, wide.shape[1])
    even = jnp.bitwise_and(sph, 1) == 0
    r6, r4, r2, r1 = (
        peers(part, "sph", masks)
        for masks in ((10, 14), (12, 8), (4, 6), (4, 2))
    )
    uh, ul, qr, th, tl = prepare(
        positions, wave_grid, vertical, reflection, projector, t_matrix
    )
    part = (jnp.where(even, part, r1) + r6) + (r2 + r4)
    other = swap(part, "sph", 1)
    size = lax.axis_size("sph")
    links = [(i, (i + 1) % size) for i in range(1, size, 2)]
    far = lax.ppermute(mine, "sph", links + [(j, i) for i, j in links])

    keep, to1, to2, to3 = project(part, other, qr, uh, ul, 4)
    got2, got1, got3 = (swap(x, "wave", mask) for x, mask in ((to2, 2), (to1, 1), (to3, 3)))
    translated = translate(
        own[None],
        slot[None],
        ((sph - 1) * block)[None],
        jnp.bitwise_and(sph, 1)[None],
        near,
        mine,
        far,
        incident,
        neighbour_index,
        link_class,
        link_count,
        translation,
    )
    summed = ((keep + translated) + got1) + (got2 + got3)
    across = swap(summed, "wave", 4)
    updated = apply_types(summed, across, sphere_type, th, tl)
    from2, from1, from3 = (swap(updated, "wave", mask) for mask in (2, 1, 3))
    return place(flip[None], (updated, from1, from2, from3))


def solution(mesh):
    placed = (
        P(None, None, "sph"),
        P(None, None, "sph"),
        P(None, "sph"),
        P(None, "sph"),
        P(None, "sph"),
        P("sph"),
        P("sph"),
        P(),
        P(),
        P(None, "wave"),
        P("wave"),
        P(None, None, None, "wave"),
        P(None, None, None, "wave"),
        P(None, None, None, "wave"),
    )

    return jax.shard_map(
        per_device, mesh=mesh, in_specs=placed, out_specs=P(None, None, "sph"), check_vma=False
    )
```
